256 devices in a mesh: cell: 64 (over x, z_hi, y, core), cls: 4 (over z_lo).
Axes of the slice: x: 4, y: 4, z: 8 (z_hi: 2, z_lo: 4; z = z_hi * 4 + z_lo), core: 2. Of those that a mesh axis runs over, the one named last changes fastest.
Arguments:
- melt: float32 [64, 32, 65536], P(None, 'cls', 'cell'), may hold values from 0 to 1
- counts: int32 [32, 65536], P('cls', 'cell'), may hold values from 0 to 800, as said below
- pressure: float32 [256, 256], P(('cell', 'cls')), may hold values from 0.5 to 2
- propagator: float32 [32, 64, 64], replicated, as said below
- coupling: float32 [32, 64], replicated, may hold values from 0.05 to 0.5
- flux_weights: float32 [32, 64], replicated, may hold values from 0.002 to 0.2
Outputs:
- shells_out: float32 [64, 32, 65536], P(None, 'cls', 'cell')
- pressure_out: float32 [256, 256], P(('cell', 'cls'))
The draws below stay inside these ranges and needn't reach their ends.
Inputs may be any that keep to these rules, and one draw needn't show every extreme that they name: counts in layer l are non-negative and below 201 + (600 * l) // 255. Each propagator matrix has a dominant diagonal.
All inputs are finite; a program needn't handle non-finite values.
Results may differ from the reference program's by a relative error of at most 0.0001.
Values sent between devices are 32-bit elements; how exact they have to be, the bound alone decides.
A program may use at most 64 MiB of HBM per device.

```python
import math
import jax
import jax.numpy as jnp
from jax import lax

NODES = 64
CLASSES = 32
SIDE = 16
SUBSTEPS = 4
PLANE = 256
NZ = 256
NCELLS = 65536


def draw_counts(key, part):
    layer = jnp.arange(NCELLS, dtype=jnp.int32) // PLANE
    upper = 201 + 600 * layer // (NZ - 1)
    upper = jnp.broadcast_to(upper[None, :], (CLASSES, NCELLS))
    values = jax.random.randint(key, (CLASSES, NCELLS), 0, upper).astype(jnp.int32)
    class_idx = jnp.arange(CLASSES, dtype=jnp.int32)[:, None]
    cell_idx = jnp.arange(NCELLS, dtype=jnp.int32)[None, :]
    at_top = jnp.logical_and(class_idx == 0, cell_idx == NCELLS - 1)
    return jnp.where(at_top, jnp.int32(800), values).astype(jnp.int32)


def draw_propagator(key, part):
    first, second = jax.random.split(jax.random.fold_in(key, 7))
    diag_vals = jax.random.uniform(first, (CLASSES, NODES, 1), jnp.float32, 0.5, 0.9)
    off_vals = jnp.clip(0.005 * jax.random.normal(second, (CLASSES, NODES, NODES), jnp.float32), -0.007, 0.007)
    rows = jnp.arange(NODES)[:, None]
    cols = jnp.arange(NODES)[None, :]
    return jnp.where((rows == cols)[None, :, :], diag_vals, off_vals).astype(jnp.float32)


def level_of(own_key, dims, pieces, low, top_value):
    factor_of = 1.0
    for axis_at, blocks in pieces:
        heights = jax.random.uniform(jax.random.fold_in(jax.random.fold_in(own_key, 6), axis_at), (blocks,), jnp.float32, low / len(pieces), top_value / len(pieces))
        factor_of = factor_of * jnp.repeat(jnp.exp(heights), dims[axis_at] // blocks).reshape((-1,) + (1,) * (len(dims) - 1 - axis_at))
    return factor_of


def setup_inputs(seed: int = 0) -> dict:
    seeds = jax.random.split(jax.random.key(seed), 7)
    melt = jnp.clip(1.0 * jax.random.uniform(seeds[0], (NODES, CLASSES, NCELLS), jnp.float32) ** level_of(seeds[0], (NODES, CLASSES, NCELLS), ((1, 4), (2, 64)), -0.2, 0.2), 0.0, 1.0)
    counts = draw_counts(jax.random.fold_in(seeds[6], 71), 0)
    pressure = jnp.clip(0.5 + 1.5 * jax.random.uniform(seeds[2], (NZ, PLANE), jnp.float32) ** level_of(seeds[2], (NZ, PLANE), ((0, 256),), -0.2, 0.2), 0.5, 2.0)
    propagator = draw_propagator(jax.random.fold_in(seeds[6], 71), 0)
    coupling = jnp.clip(jnp.exp(jax.random.uniform(seeds[4], (CLASSES, NODES), jnp.float32, math.log(0.05), math.log(0.5))), 0.05, 0.5)
    flux_weights = jnp.clip(jnp.exp(jax.random.uniform(seeds[5], (CLASSES, NODES), jnp.float32, math.log(0.002), math.log(0.2))), 0.002, 0.2)
    return dict(melt=melt, counts=counts, pressure=pressure, propagator=propagator, coupling=coupling, flux_weights=flux_weights)


count_scale = 400.0


def reference(melt, counts, pressure, propagator, coupling, flux_weights):
    counts_f = counts.astype(jnp.float32)
    for step in range(SUBSTEPS):
        wall = 0.5 * pressure.reshape(NCELLS)
        melt = jnp.einsum('kij,jkc->ikc', propagator, melt, precision=lax.Precision.HIGHEST) + coupling.T[:, :, None] * wall[None, None, :]
        flux = jnp.einsum('ki,ikc->kc', flux_weights, melt, precision=lax.Precision.HIGHEST)
        gas = jnp.sum(counts_f * flux, axis=0) / (count_scale * CLASSES)
        chamber = 1.5 - 0.5 * jnp.sum(gas) / NCELLS
        field = pressure.reshape(NZ, SIDE, SIDE)
        padded = jnp.pad(field, 1)
        lap = padded[2:, 1:-1, 1:-1] + padded[:-2, 1:-1, 1:-1] + padded[1:-1, 2:, 1:-1] + padded[1:-1, :-2, 1:-1] + padded[1:-1, 1:-1, 2:] + padded[1:-1, 1:-1, :-2] - 6.0 * field
        field = field + 0.15 * lap + 0.1 * gas.reshape(NZ, SIDE, SIDE) + 0.2 * (chamber - field)
        pressure = field.reshape(NZ, PLANE)
    return melt, pressure
```

```python
import functools

import jax
import jax.numpy as jnp
from jax import lax
from jax.experimental import pallas as pl
from jax.experimental.pallas import tpu as pltpu
from jax.sharding import PartitionSpec as P

MESH = pl.DeviceIdType.MESH
F32 = jnp.float32
BF16 = jnp.bfloat16
NODES = 64
CLASSES = 32
SIDE = 16
PLANE = 256
LAYERS = 4
BLOCK = LAYERS * PLANE
KC = 8
NCELLS = 65536
COUNT_SCALE = 400.0
CHUNKS = 8


def split2(x):
    hi = x.astype(BF16)
    return hi, (x - hi.astype(F32)).astype(BF16)


def dot_nn(a, b):
    return jnp.dot(a, b, preferred_element_type=F32)


def dot3(a, b):
    (ah, al), (bh, bl) = a, b
    return dot_nn(ah, bh) + (dot_nn(al, bh) + dot_nn(ah, bl))


def main_kernel(
    melt_hbm, counts_hbm, pres_ref, prop_hbm, coup_hbm, fw_hbm,
    m_ref, walls_ref, vec_ref, pout_ref,
    melt_v, counts_ref, prop_v, coup_v, fw_v, part, p0, acc_a, acc_b, srow, pbuf,
    load_sem, small_sem, part_send, part_recv, p_send, p_recv, a_send, a_recv, b_send, b_recv,
):
    cell = lax.axis_index("cell")
    cls = lax.axis_index("cls")
    core = cell % 2
    yy = (cell // 2) % 4
    zh = (cell // 8) % 2
    xx = cell // 16
    has_prev = cell > 0
    has_next = cell < 63

    loads = [
        pltpu.make_async_copy(melt_hbm.at[:, pl.ds(i * 128, 128)], melt_v.at[i], load_sem.at[i])
        for i in range(CHUNKS)
    ]
    smalls = [
        pltpu.make_async_copy(prop_hbm.at[pl.ds(cls * 512, 512)], prop_v, small_sem.at[0]),
        pltpu.make_async_copy(coup_hbm.at[pl.ds(cls * 8, 8)], coup_v, small_sem.at[1]),
        pltpu.make_async_copy(fw_hbm.at[pl.ds(cls * 8, 8)], fw_v, small_sem.at[2]),
        pltpu.make_async_copy(counts_hbm, counts_ref, small_sem.at[3]),
        pltpu.make_async_copy(pres_ref, p0.at[1, cls], small_sem.at[4]),
    ]
    for copy in smalls + loads:
        copy.start()

    barrier = pltpu.get_barrier_semaphore()

    def signal(c, k):
        pl.semaphore_signal(barrier, inc=1, device_id=(c, k), device_id_type=MESH)

    def stage_a_peer(d):
        s = (yy * 2 + core + d) % 8
        return (cell // 8) * 8 + s

    def block_at(x, z, y, c):
        return ((x * 2 + z) * 4 + y) * 2 + c

    is_edge = jnp.logical_or(cls == 0, cls == 3)
    near = jnp.where(cls == 3, 0, 3)
    near2 = jnp.where(cls == 3, 1, 2)
    source = jnp.where(cls < 2, 3, 0)

    for d in range(1, 4):
        signal(cell, (cls + d) % 4)
    for d in range(1, 8):
        signal(stage_a_peer(d), cls)
    for d in range(1, 4):
        signal(block_at((xx + d) % 4, zh, yy, core), cls)
    for d in range(4):
        signal(block_at((xx + d) % 4, 1 - zh, yy, core), source)

    @pl.when(has_prev)
    def _():
        for k in range(4):
            signal(cell - 1, k)

    @pl.when(has_next)
    def _():
        for k in range(4):
            signal(cell + 1, k)

    one = jnp.int32(1)
    greeted = 13 + 8 * jnp.where(is_edge, one, 0) + 4 * jnp.where(has_prev, one, 0) + 4 * jnp.where(has_next, one, 0)
    pl.semaphore_wait(barrier, greeted)

    def p_copy(rel, d, c, k):
        return pltpu.make_async_remote_copy(
            src_ref=pres_ref, dst_ref=p0.at[rel, cls], send_sem=p_send.at[rel, d],
            recv_sem=p_recv.at[rel, cls], device_id=(c, k), device_id_type=MESH)

    def part_copy(rel, d, c, k):
        lo = {0: PLANE, 1: 0, 2: 0}[rel]
        n = {0: 3 * PLANE, 1: BLOCK, 2: 3 * PLANE}[rel]
        return pltpu.make_async_remote_copy(
            src_ref=part.at[1, cls, :, pl.ds(lo, n)], dst_ref=part.at[rel, cls, :, pl.ds(lo, n)],
            send_sem=part_send.at[rel, d], recv_sem=part_recv.at[rel, cls],
            device_id=(c, k), device_id_type=MESH)

    def send_all(make):
        for d in range(1, 4):
            make(1, d, cell, (cls + d) % 4).start()

        @pl.when(has_prev)
        def _():
            for k in range(4):
                make(2, k, cell - 1, k).start()

        @pl.when(has_next)
        def _():
            for k in range(4):
                make(0, k, cell + 1, k).start()

    def wait_sends(make):
        for d in range(1, 4):
            make(1, d, cell, (cls + d) % 4).wait_send()

        @pl.when(has_prev)
        def _():
            for k in range(4):
                make(2, k, cell - 1, k).wait_send()

        @pl.when(has_next)
        def _():
            for k in range(4):
                make(0, k, cell + 1, k).wait_send()

    def p_arrival(rel, k):
        return pltpu.make_async_copy(p0.at[rel, k], p0.at[rel, k], p_recv.at[rel, k])

    def part_arrival(rel, k):
        lo = {0: PLANE, 1: 0, 2: 0}[rel]
        n = {0: 3 * PLANE, 1: BLOCK, 2: 3 * PLANE}[rel]
        ref = part.at[rel, k, :, pl.ds(lo, n)]
        return pltpu.make_async_copy(ref, ref, part_recv.at[rel, k])

    def wait_arrivals(arrival):
        for d in range(1, 4):
            arrival(1, (cls + d) % 4).wait()

        @pl.when(has_prev)
        def _():
            for k in range(4):
                arrival(0, k).wait()

        @pl.when(has_next)
        def _():
            for k in range(4):
                arrival(2, k).wait()

    send_all(p_copy)

    @pl.when(jnp.logical_not(has_prev))
    def _():
        p0[0] = jnp.zeros((4, 1, PLANE), F32)
        part[0] = jnp.zeros((4, KC, BLOCK), F32)

    @pl.when(jnp.logical_not(has_next))
    def _():
        p0[2] = jnp.zeros((4, 1, PLANE), F32)
        part[2] = jnp.zeros((4, KC, BLOCK), F32)

    for copy in smalls:
        copy.wait()
    prop = prop_v[...]
    p_hi, p_lo = split2(prop)
    pp = jnp.concatenate([p_hi, p_lo], axis=1)
    lane = lax.broadcasted_iota(jnp.int32, (KC, 128), 1)
    row = lax.broadcasted_iota(jnp.int32, (KC, 128), 0)
    half = jnp.where(lane >= 64, 1, 0)

    def doubled(x):
        return jnp.concatenate([x, x], axis=1)

    def kron(x):
        return jnp.concatenate([jnp.where(row == 2 * v + half, x, 0.0) for v in range(4)], axis=1)

    def row_step(r):
        hi, lo = split2(kron(r))
        y = dot_nn(jnp.concatenate([hi, lo], axis=0), pp)
        y = y[:KC] + y[KC:]
        return y + pltpu.roll(y, 64, 1)

    fw = fw_v[...]
    coup = coup_v[...]
    rs = [doubled(fw)]
    for t in range(4):
        rs.append(row_step(rs[-1]))

    counts_f = counts_ref[...].astype(F32)
    for i, copy in enumerate(loads):
        copy.wait()
    acc = [[jnp.zeros((KC, 128), F32) for _ in range(CHUNKS)] for _ in range(4)]
    for j in range(NODES):
        factors = [jnp.broadcast_to(rs[t + 1][:, j : j + 1], (KC, 128)) for t in range(4)]
        for i in range(CHUNKS):
            node = melt_v[i, pl.ds(j * KC, KC), :]
            for t in range(4):
                acc[t][i] = acc[t][i] + factors[t] * node
    scale = 1.0 / (COUNT_SCALE * CLASSES)
    for t in range(4):
        flux = jnp.concatenate(acc[t], axis=1)
        part[1, cls, t : t + 1, :] = jnp.sum(counts_f * flux, axis=0, keepdims=True) * scale
        a_t = jnp.sum(rs[t][:, :NODES] * coup, axis=1, keepdims=True)
        part[1, cls, 4 + t : 5 + t, :] = jnp.sum(counts_f * a_t, axis=0, keepdims=True) * scale

    send_all(part_copy)

    def col_step(v):
        hi, lo = split2(v[:, :NODES])
        lhs = jnp.concatenate([hi, lo], axis=0)
        nt = (((1,), (1,)), ((), ()))
        y = lax.dot_general(lhs, p_hi, nt, preferred_element_type=F32)
        y = y[:KC] + y[KC:] + lax.dot_general(hi, p_lo, nt, preferred_element_type=F32)
        z = jnp.zeros((KC, 128), F32)
        for q in range(4):
            z = z + jnp.where(row == 2 * q + half, y[:, 128 * q : 128 * (q + 1)], 0.0)
        return z + pltpu.roll(z, 64, 1)

    vs = [doubled(coup)]
    for s in range(3):
        vs.append(col_step(vs[-1]))
    for s in range(4):
        for j in range(NODES):
            vec_ref[s, pl.ds(j * KC, KC), :] = jnp.broadcast_to(vs[3 - s][:, j : j + 1], (KC, 128))

    for k in range(KC):
        one = split2(prop[k * NODES : (k + 1) * NODES, :])
        two = split2(dot3(one, one))
        four_hi, four_lo = split2(dot3(two, two))
        lhs = jnp.concatenate([four_hi, four_lo], axis=0)

        def columns(n, carry, lhs=lhs, four_hi=four_hi, k=k):
            at = pl.ds(k, NODES, stride=KC)
            x_hi, x_lo = split2(melt_v[n, at, :])
            y = dot_nn(lhs, x_hi)
            m_ref[n, at, :] = y[:NODES] + y[NODES:] + dot_nn(four_hi, x_lo)
            return carry

        lax.fori_loop(0, BLOCK // 128, columns, 0)

    wait_arrivals(p_arrival)
    wait_arrivals(part_arrival)
    inside = [jnp.where(has_prev, 1.0, 0.0).astype(F32), None, jnp.where(has_next, 1.0, 0.0).astype(F32)]
    totals = [part[b, 0] + part[b, 1] + (part[b, 2] + part[b, 3]) for b in range(3)]

    lane2 = lax.broadcasted_iota(jnp.int32, (KC, PLANE), 1)
    row2 = lax.broadcasted_iota(jnp.int32, (KC, PLANE), 0)

    def field(layer, r):
        b, l = divmod(layer + 4, 4)
        return jnp.broadcast_to(totals[b][r : r + 1, l * PLANE : (l + 1) * PLANE], (KC, PLANE))

    def plane_neighbours(x):
        west = jnp.where(lane2 % SIDE == 0, 0.0, pltpu.roll(x, 1, 1))
        east = jnp.where(lane2 % SIDE == SIDE - 1, 0.0, pltpu.roll(x, PLANE - 1, 1))
        north = jnp.where(lane2 < SIDE, 0.0, pltpu.roll(x, SIDE, 1))
        south = jnp.where(lane2 >= PLANE - SIDE, 0.0, pltpu.roll(x, PLANE - SIDE, 1))
        return west + east + (north + south)

    states = [{}]
    for layer in range(-4, 8):
        b, l = divmod(layer + 4, 4)
        states[0][layer] = jnp.where(row2 == 0, jnp.broadcast_to(p0[b, l], (KC, PLANE)), 0.0)
    gases = []
    fields = {}

    def field_of(layer, r):
        if (layer, r) not in fields:
            fields[layer, r] = field(layer, r)
        return fields[layer, r]

    for s in range(4):
        gas = {}
        reach = 3 - s
        for layer in range(-reach, LAYERS + reach):
            g = jnp.where(row2 == 0, field_of(layer, s), 0.0)
            for m in range(s + 1):
                g = g + field_of(layer, 4 + m) * (0.5 * states[s - m][layer])
            gas[layer] = g
        gases.append(gas)
        new = {}
        for layer in range(-reach, LAYERS + reach):
            x = states[s][layer]
            around = plane_neighbours(x) + (states[s][layer - 1] + states[s][layer + 1])
            x = x + 0.15 * (around - 6.0 * x) + 0.1 * gas[layer] - 0.2 * x
            x = x + jnp.where(row2 == s + 1, 0.2, 0.0)
            if layer < 0:
                x = x * inside[0]
            if layer >= LAYERS:
                x = x * inside[2]
            new[layer] = x
        states.append(new)

    packed = jnp.zeros((KC, 128), F32)
    for s in range(4):
        t = gases[s][0] + gases[s][1] + (gases[s][2] + gases[s][3])
        t = jnp.sum(t[:, :128] + t[:, 128:], axis=1, keepdims=True)
        packed = packed + jnp.where(jnp.logical_and(lane == s * 4 + row, row < 4), t, 0.0)
    packed = jnp.sum(packed, axis=0, keepdims=True)
    slot_a = yy * 2 + core
    slot_b = xx * 2 + zh
    srow[0] = packed
    acc_a[slot_a] = packed

    def a_copy(d):
        return pltpu.make_async_remote_copy(
            src_ref=srow.at[0], dst_ref=acc_a.at[slot_a], send_sem=a_send.at[d],
            recv_sem=a_recv.at[slot_a], device_id=(stage_a_peer(d), cls), device_id_type=MESH)

    for d in range(1, 8):
        a_copy(d).start()
    for d in range(1, 8):
        s = (slot_a + d) % 8
        pltpu.make_async_copy(acc_a.at[s], acc_a.at[s], a_recv.at[s]).wait()
    total = acc_a[0]
    for s in range(1, 8):
        total = total + acc_a[s]
    srow[1] = total
    acc_b[slot_b] = total

    def b_copy(i, x, z, k):
        return pltpu.make_async_remote_copy(
            src_ref=srow.at[1], dst_ref=acc_b.at[slot_b], send_sem=b_send.at[i],
            recv_sem=b_recv.at[slot_b], device_id=(block_at(x, z, yy, core), k), device_id_type=MESH)

    same = [b_copy(d, (xx + d) % 4, zh, cls) for d in range(1, 4)]
    across = [
        b_copy(4 + 2 * d + e, (xx + d) % 4, 1 - zh, k) for d in range(4) for e, k in ((0, near), (1, near2))
    ]

    @pl.when(is_edge)
    def _():
        for copy in across:
            copy.start()

    for copy in same:
        copy.start()
    for d in range(1, 8):
        s = (slot_b + d) % 8
        pltpu.make_async_copy(acc_b.at[s], acc_b.at[s], b_recv.at[s]).wait()
    total = acc_b[0]
    for s in range(1, 8):
        total = total + acc_b[s]

    def coefficient(s, r):
        return total[:, s * 4 + r : s * 4 + r + 1]

    chambers = []
    for s in range(4):
        t = coefficient(s, 0)
        for r in range(s):
            t = t + chambers[r] * coefficient(s, r + 1)
        chambers.append(1.5 - 0.5 * (t / NCELLS))
    weights = jnp.where(row2 == 0, 1.0, 0.0)
    for r in range(3):
        weights = jnp.where(row2 == r + 1, chambers[r], weights)

    for layer in range(LAYERS):
        at = pl.ds(layer * PLANE, PLANE)
        for s in range(4):
            walls_ref[s : s + 1, at] = 0.5 * jnp.sum(weights * states[s][layer], axis=0, keepdims=True)
        pbuf[layer] = jnp.sum(weights * states[4][layer], axis=0, keepdims=True) + 0.2 * chambers[3]
    pout_ref[...] = pbuf[cls]

    wait_sends(p_copy)
    wait_sends(part_copy)
    for d in range(1, 8):
        a_copy(d).wait_send()

    @pl.when(is_edge)
    def _():
        for copy in across:
            copy.wait_send()

    for copy in same:
        copy.wait_send()


def finish_kernel(m_ref, walls_ref, vec_ref, p_ref, out_hbm, pout_ref, out_v, sem):
    pout_ref[...] = p_ref[...]
    copies = []
    for i in range(CHUNKS):
        walls = [jnp.broadcast_to(walls_ref[s : s + 1, i * 128 : (i + 1) * 128], (KC, 128)) for s in range(4)]
        for j in range(NODES):
            at = pl.ds(j * KC, KC)
            y = m_ref[i, at, :]
            for s in range(4):
                y = y + vec_ref[s, at, :] * walls[s]
            out_v[i, at, :] = y
        copies.append(pltpu.make_async_copy(out_v.at[i], out_hbm.at[:, pl.ds(i * 128, 128)], sem.at[i]))
        copies[-1].start()
    for copy in copies:
        copy.wait()


def shards(melt, counts, pressure, propagator, coupling, flux_weights):
    vmem = pl.BlockSpec(memory_space=pltpu.VMEM)
    hbm = pl.BlockSpec(memory_space=pltpu.HBM)
    dma = pltpu.SemaphoreType.DMA
    m, walls, vec, pout = pl.pallas_call(
        main_kernel,
        name="block_step",
        out_shape=(
            jax.ShapeDtypeStruct((CHUNKS, NODES * KC, 128), F32),
            jax.ShapeDtypeStruct((4, BLOCK), F32),
            jax.ShapeDtypeStruct((4, NODES * KC, 128), F32),
            jax.ShapeDtypeStruct((1, PLANE), F32),
        ),
        in_specs=[hbm] * 6,
        out_specs=(vmem, vmem, vmem, vmem),
        scratch_shapes=[
            pltpu.VMEM((CHUNKS, NODES * KC, 128), F32),
            pltpu.VMEM((KC, BLOCK), jnp.int32),
            pltpu.VMEM((KC * NODES, NODES), F32),
            pltpu.VMEM((KC, NODES), F32),
            pltpu.VMEM((KC, NODES), F32),
            pltpu.VMEM((3, 4, KC, BLOCK), F32),
            pltpu.VMEM((3, 4, 1, PLANE), F32),
            pltpu.VMEM((8, 1, 128), F32),
            pltpu.VMEM((8, 1, 128), F32),
            pltpu.VMEM((2, 1, 128), F32),
            pltpu.VMEM((LAYERS, 1, PLANE), F32),
            dma((CHUNKS,)), dma((5,)),
            dma((3, 4)), dma((3, 4)), dma((3, 4)), dma((3, 4)),
            dma((8,)), dma((8,)), dma((12,)), dma((8,)),
        ],
        compiler_params=pltpu.CompilerParams(collective_id=0, has_side_effects=True, vmem_limit_bytes=32 << 20),
    )(
        *(
            pltpu.with_memory_space_constraint(x, pltpu.HBM)
            for x in (
                melt.reshape(NODES * KC, BLOCK), counts, pressure,
                propagator.reshape(CLASSES * NODES, NODES), coupling, flux_weights,
            )
        )
    )
    shells, pout = pl.pallas_call(
        finish_kernel,
        name="walls_into_shells",
        out_shape=(
            jax.ShapeDtypeStruct((NODES * KC, BLOCK), F32),
            jax.ShapeDtypeStruct((1, PLANE), F32),
        ),
        in_specs=[vmem, vmem, vmem, vmem],
        out_specs=(hbm, vmem),
        scratch_shapes=[pltpu.VMEM((CHUNKS, NODES * KC, 128), F32), dma((CHUNKS,))],
        compiler_params=pltpu.CompilerParams(vmem_limit_bytes=32 << 20),
    )(m, walls, vec, pout)
    return shells.reshape(NODES, KC, BLOCK), pout


def solution(mesh):
    placed = (P(None, "cls", "cell"), P("cls", "cell"), P(("cell", "cls"), None), P(), P(), P())
    return jax.shard_map(
        shards,
        mesh=mesh,
        in_specs=placed,
        out_specs=(P(None, "cls", "cell"), P(("cell", "cls"), None)),
        check_vma=False,
    )
```

```python
import functools

import jax
import jax.numpy as jnp
from jax import lax
from jax.experimental import pallas as pl
from jax.experimental.pallas import tpu as pltpu
from jax.sharding import PartitionSpec as P

MESH = pl.DeviceIdType.MESH
F32 = jnp.float32
BF16 = jnp.bfloat16
NODES = 64
CLASSES = 32
SIDE = 16
PLANE = 256
LAYERS = 4
BLOCK = LAYERS * PLANE
KC = 8
NCELLS = 65536
COUNT_SCALE = 400.0
CHUNKS = 8
GROUPS = 8


class Many:
    def __init__(self, copies):
        self.copies = copies

    def start(self):
        for copy in self.copies:
            copy.start()

    def wait(self):
        for copy in self.copies:
            copy.wait()

    def wait_send(self):
        for copy in self.copies:
            copy.wait_send()


def split2(x):
    hi = x.astype(BF16)
    return hi, (x - hi.astype(F32)).astype(BF16)


def dot_nn(a, b):
    return jnp.dot(a, b, preferred_element_type=F32)


def dot3(a, b):
    (ah, al), (bh, bl) = a, b
    return dot_nn(ah, bh) + (dot_nn(al, bh) + dot_nn(ah, bl))


def main_kernel(
    melt_hbm, counts_hbm, pres_ref, prop_hbm, coup_hbm, fw_hbm,
    m_ref, walls_ref, vec_ref, pout_ref,
    melt_v, melt_hi, counts_ref, prop_v, coup_v, fw_v, part, p0, acc, srow, pbuf,
    load_sem, small_sem, part_send, part_recv, p_send, p_recv, s_send, s_recv, ready,
):
    cell = lax.axis_index("cell")
    cls = lax.axis_index("cls")
    core = cell % 2
    yy = (cell // 2) % 4
    zh = (cell // 8) % 2
    xx = cell // 16
    has_prev = cell > 0
    has_next = cell < 63

    loads = [
        pltpu.make_async_copy(melt_hbm.at[:, pl.ds(i * 128, 128)], melt_v.at[i], load_sem.at[i])
        for i in range(CHUNKS)
    ]
    smalls = [
        pltpu.make_async_copy(prop_hbm.at[pl.ds(cls * 512, 512)], prop_v, small_sem.at[0]),
        pltpu.make_async_copy(coup_hbm.at[pl.ds(cls * 8, 8)], coup_v, small_sem.at[1]),
        pltpu.make_async_copy(fw_hbm.at[pl.ds(cls * 8, 8)], fw_v, small_sem.at[2]),
        pltpu.make_async_copy(counts_hbm, counts_ref, small_sem.at[3]),
        pltpu.make_async_copy(pres_ref, p0.at[1, cls], small_sem.at[4]),
    ]
    for copy in smalls + loads:
        copy.start()

    barrier = pltpu.get_barrier_semaphore()

    def signal(c, k):
        pl.semaphore_signal(barrier, inc=1, device_id=(c, k), device_id_type=MESH)

    def stage_a_peer(d):
        s = (yy * 2 + core + d) % 8
        return (cell // 8) * 8 + s

    def block_at(x, z, y, c):
        return ((x * 2 + z) * 4 + y) * 2 + c

    is_edge = jnp.logical_or(cls == 0, cls == 3)
    near = jnp.where(cls == 3, 0, 3)
    near2 = jnp.where(cls == 3, 1, 2)
    source = jnp.where(cls < 2, 3, 0)

    for d in range(1, 4):
        signal(cell, (cls + d) % 4)
    for d in range(1, 8):
        signal(stage_a_peer(d), cls)
    for d in range(1, 4):
        signal(block_at((xx + d) % 4, zh, yy, core), cls)
    for d in range(4):
        signal(block_at((xx + d) % 4, 1 - zh, yy, core), source)

    @pl.when(is_edge)
    def _():
        for d in range(4):
            signal(block_at((xx + d) % 4, 1 - zh, yy, core), near2)

    @pl.when(has_prev)
    def _():
        for k in range(4):
            signal(cell - 1, k)

    @pl.when(has_next)
    def _():
        for k in range(4):
            signal(cell + 1, k)

    def p_copy(rel, d, c, k):
        return pltpu.make_async_remote_copy(
            src_ref=pres_ref, dst_ref=p0.at[rel, cls], send_sem=p_send.at[rel, d],
            recv_sem=p_recv.at[rel, cls], device_id=(c, k), device_id_type=MESH)

    def part_copies(rel, d, c, k):
        pieces = {0: ((2, 1), (4, 2), (6, 3)), 1: ((8, None),), 2: ((6, 0), (4, 1), (2, 2))}[rel]
        out = []
        for i, (n, layer) in enumerate(pieces):
            lo, size = (0, BLOCK) if layer is None else (layer * PLANE, PLANE)
            out.append(pltpu.make_async_remote_copy(
                src_ref=part.at[1, cls, pl.ds(0, n), pl.ds(lo, size)],
                dst_ref=part.at[rel, cls, pl.ds(0, n), pl.ds(lo, size)],
                send_sem=part_send.at[rel, d, i], recv_sem=part_recv.at[rel, cls, i],
                device_id=(c, k), device_id_type=MESH))
        return Many(out)

    part_copy = part_copies

    def send_all(make):
        for d in range(1, 4):
            make(1, d, cell, (cls + d) % 4).start()

        @pl.when(has_prev)
        def _():
            for k in range(4):
                make(2, k, cell - 1, k).start()

        @pl.when(has_next)
        def _():
            for k in range(4):
                make(0, k, cell + 1, k).start()

    def wait_sends(make):
        for d in range(1, 4):
            make(1, d, cell, (cls + d) % 4).wait_send()

        @pl.when(has_prev)
        def _():
            for k in range(4):
                make(2, k, cell - 1, k).wait_send()

        @pl.when(has_next)
        def _():
            for k in range(4):
                make(0, k, cell + 1, k).wait_send()

    def p_arrival(rel, k):
        return pltpu.make_async_copy(p0.at[rel, k], p0.at[rel, k], p_recv.at[rel, k])

    def part_arrival(rel, k):
        pieces = {0: ((2, 1), (4, 2), (6, 3)), 1: ((8, None),), 2: ((6, 0), (4, 1), (2, 2))}[rel]
        out = []
        for i, (n, layer) in enumerate(pieces):
            lo, size = (0, BLOCK) if layer is None else (layer * PLANE, PLANE)
            ref = part.at[rel, k, pl.ds(0, n), pl.ds(lo, size)]
            out.append(pltpu.make_async_copy(ref, ref, part_recv.at[rel, k, i]))
        return Many(out)

    def wait_arrivals(arrival):
        for d in range(1, 4):
            arrival(1, (cls + d) % 4).wait()

        @pl.when(has_prev)
        def _():
            for k in range(4):
                arrival(0, k).wait()

        @pl.when(has_next)
        def _():
            for k in range(4):
                arrival(2, k).wait()


    @pl.when(jnp.logical_not(has_prev))
    def _():
        p0[0] = jnp.zeros((4, 1, PLANE), F32)
        part[0] = jnp.zeros((4, KC, BLOCK), F32)

    @pl.when(jnp.logical_not(has_next))
    def _():
        p0[2] = jnp.zeros((4, 1, PLANE), F32)
        part[2] = jnp.zeros((4, KC, BLOCK), F32)

    for copy in smalls:
        copy.wait()
    prop = prop_v[...]
    p_hi, p_lo = split2(prop)
    pp = jnp.concatenate([p_hi, p_lo], axis=1)
    lane = lax.broadcasted_iota(jnp.int32, (KC, 128), 1)
    row = lax.broadcasted_iota(jnp.int32, (KC, 128), 0)
    half = jnp.where(lane >= 64, 1, 0)

    def doubled(x):
        return jnp.concatenate([x, x], axis=1)

    def kron(x):
        return jnp.concatenate([jnp.where(row == 2 * v + half, x, 0.0) for v in range(4)], axis=1)

    def spread(r):
        return jnp.concatenate(split2(kron(r)), axis=0)

    def row_step(wide):
        y = dot_nn(wide, pp)
        y = y[:KC] + y[KC:]
        return y + pltpu.roll(y, 64, 1)

    fw = fw_v[...]
    coup = coup_v[...]
    rs = [doubled(fw)]
    wide = [spread(rs[0])]
    for t in range(4):
        rs.append(row_step(wide[-1]))
        wide.append(spread(rs[-1]))
    weights_f = jnp.concatenate(wide[1:], axis=0)

    counts_f = counts_ref[...].astype(F32)
    flux = [[] for _ in range(4)]
    for n in range(CHUNKS // 2):
        loads[2 * n].wait()
        loads[2 * n + 1].wait()
        for k in range(KC):
            at = pl.ds(k, NODES, stride=KC)
            pair = jnp.concatenate([melt_v[2 * n, at, :], melt_v[2 * n + 1, at, :]], axis=1)
            melt_hi[pl.ds(k * NODES, NODES), pl.ds(n * 256, 256)] = pair.astype(BF16)
        y = dot_nn(weights_f, melt_hi[:, pl.ds(n * 256, 256)])
        for t in range(4):
            flux[t].append(y[16 * t : 16 * t + 8] + y[16 * t + 8 : 16 * t + 16])
    scale = 1.0 / (COUNT_SCALE * CLASSES)
    for t in range(4):
        flux_t = jnp.concatenate(flux[t], axis=1)
        part[1, cls, 2 * t : 2 * t + 1, :] = jnp.sum(counts_f * flux_t, axis=0, keepdims=True) * scale
        a_t = jnp.sum(rs[t][:, :NODES] * coup, axis=1, keepdims=True)
        part[1, cls, 2 * t + 1 : 2 * t + 2, :] = jnp.sum(counts_f * a_t, axis=0, keepdims=True) * scale

    one = jnp.int32(1)
    greeted = 17 + 4 * jnp.where(is_edge, one, 0) + 4 * jnp.where(has_prev, one, 0) + 4 * jnp.where(has_next, one, 0)
    pl.semaphore_wait(barrier, greeted)

    send_all(p_copy)
    send_all(part_copy)

    def announce(c, k):
        pl.semaphore_signal(ready, inc=1, device_id=(c, k), device_id_type=MESH)

    for d in range(1, 4):
        announce(block_at((xx + d) % 4, zh, yy, core), cls)
    for d in range(4):
        announce(block_at((xx + d) % 4, 1 - zh, yy, core), source)

    def col_step(v):
        hi, lo = split2(v[:, :NODES])
        lhs = jnp.concatenate([hi, lo], axis=0)
        nt = (((1,), (1,)), ((), ()))
        y = lax.dot_general(lhs, p_hi, nt, preferred_element_type=F32)
        y = y[:KC] + y[KC:] + lax.dot_general(hi, p_lo, nt, preferred_element_type=F32)
        z = jnp.zeros((KC, 128), F32)
        for q in range(4):
            z = z + jnp.where(row == 2 * q + half, y[:, 128 * q : 128 * (q + 1)], 0.0)
        return z + pltpu.roll(z, 64, 1)

    vs = [doubled(coup)]
    for s in range(3):
        vs.append(col_step(vs[-1]))
    for s in range(4):
        for j in range(NODES):
            vec_ref[s, pl.ds(j * KC, KC), :] = jnp.broadcast_to(vs[3 - s][:, j : j + 1], (KC, 128))

    for k in range(KC):
        base = split2(prop[k * NODES : (k + 1) * NODES, :])
        two = split2(dot3(base, base))
        four_hi, four_lo = split2(dot3(two, two))
        lhs = jnp.concatenate([four_hi, four_hi, four_lo], axis=1)
        at = pl.ds(k, NODES, stride=KC)
        for n in range(CHUNKS // 2):
            x = jnp.concatenate([melt_v[2 * n, at, :], melt_v[2 * n + 1, at, :]], axis=1)
            x_hi = melt_hi[pl.ds(k * NODES, NODES), pl.ds(n * 256, 256)]
            x_lo = (x - x_hi.astype(F32)).astype(BF16)
            y = dot_nn(lhs, jnp.concatenate([x_hi, x_lo, x_hi], axis=0))
            m_ref[2 * n, at, :] = y[:, :128]
            m_ref[2 * n + 1, at, :] = y[:, 128:]

    wait_arrivals(p_arrival)
    wait_arrivals(part_arrival)
    inside = [jnp.where(has_prev, 1.0, 0.0).astype(F32), None, jnp.where(has_next, 1.0, 0.0).astype(F32)]
    totals = [part[b, 0] + part[b, 1] + (part[b, 2] + part[b, 3]) for b in range(3)]

    lane2 = lax.broadcasted_iota(jnp.int32, (KC, PLANE), 1)
    row2 = lax.broadcasted_iota(jnp.int32, (KC, PLANE), 0)

    def field(layer, r):
        b, l = divmod(layer + 4, 4)
        return jnp.broadcast_to(totals[b][r : r + 1, l * PLANE : (l + 1) * PLANE], (KC, PLANE))

    def plane_neighbours(x):
        west = jnp.where(lane2 % SIDE == 0, 0.0, pltpu.roll(x, 1, 1))
        east = jnp.where(lane2 % SIDE == SIDE - 1, 0.0, pltpu.roll(x, PLANE - 1, 1))
        north = jnp.where(lane2 < SIDE, 0.0, pltpu.roll(x, SIDE, 1))
        south = jnp.where(lane2 >= PLANE - SIDE, 0.0, pltpu.roll(x, PLANE - SIDE, 1))
        return west + east + (north + south)

    states = [{}]
    for layer in range(-4, 8):
        b, l = divmod(layer + 4, 4)
        states[0][layer] = jnp.where(row2 == 0, jnp.broadcast_to(p0[b, l], (KC, PLANE)), 0.0)
    gases = []
    fields = {}

    def field_of(layer, r):
        if (layer, r) not in fields:
            fields[layer, r] = field(layer, r)
        return fields[layer, r]

    for s in range(4):
        gas = {}
        reach = 3 - s
        for layer in range(-reach, LAYERS + reach):
            g = jnp.where(row2 == 0, field_of(layer, 2 * s), 0.0)
            for m in range(s + 1):
                g = g + field_of(layer, 2 * m + 1) * (0.5 * states[s - m][layer])
            gas[layer] = g
        gases.append(gas)
        new = {}
        for layer in range(-reach, LAYERS + reach):
            x = states[s][layer]
            around = plane_neighbours(x) + (states[s][layer - 1] + states[s][layer + 1])
            x = x + 0.15 * (around - 6.0 * x) + 0.1 * gas[layer] - 0.2 * x
            x = x + jnp.where(row2 == s + 1, 0.2, 0.0)
            if layer < 0:
                x = x * inside[0]
            if layer >= LAYERS:
                x = x * inside[2]
            new[layer] = x
        states.append(new)

    packed = jnp.zeros((KC, 128), F32)
    for s in range(4):
        t = gases[s][0] + gases[s][1] + (gases[s][2] + gases[s][3])
        t = jnp.sum(t[:, :128] + t[:, 128:], axis=1, keepdims=True)
        packed = packed + jnp.where(jnp.logical_and(lane == s * 4 + row, row < 4), t, 0.0)
    packed = jnp.sum(packed, axis=0, keepdims=True)
    slot = (xx * 4 + yy) * 2 + core
    srow[0] = packed
    acc[zh * 32 + slot] = packed
    pl.semaphore_wait(ready, 3 + 8 * jnp.where(is_edge, one, 0))

    def sum_copy(t, z, k, sem, arrived):
        return pltpu.make_async_remote_copy(
            src_ref=srow.at[0], dst_ref=acc.at[zh * 32 + slot], send_sem=sem, recv_sem=arrived,
            device_id=((t // 8) * 16 + z * 8 + t % 8, k), device_id_type=MESH)

    @pl.when(is_edge)
    def _():
        def across(d, carry):
            t = (slot + d) % 32
            sum_copy(t, 1 - zh, near, s_send.at[1], s_recv.at[1]).start()
            sum_copy(t, 1 - zh, near2, s_send.at[2], s_recv.at[1]).start()
            return carry

        lax.fori_loop(0, 32, across, 0)

    def same(d, carry):
        sum_copy((slot + d) % 32, zh, cls, s_send.at[0], s_recv.at[0]).start()
        return carry

    lax.fori_loop(1, 32, same, 0)
    first31 = acc.at[pl.ds(0, 31)]
    first32 = acc.at[pl.ds(0, 32)]
    pltpu.make_async_copy(first31, first31, s_recv.at[0]).wait()
    pltpu.make_async_copy(first32, first32, s_recv.at[1]).wait()
    total = jnp.sum(acc[...], axis=0)

    def coefficient(s, r):
        return total[:, s * 4 + r : s * 4 + r + 1]

    chambers = []
    for s in range(4):
        t = coefficient(s, 0)
        for r in range(s):
            t = t + chambers[r] * coefficient(s, r + 1)
        chambers.append(1.5 - 0.5 * (t / NCELLS))
    weights = jnp.where(row2 == 0, 1.0, 0.0)
    for r in range(3):
        weights = jnp.where(row2 == r + 1, chambers[r], weights)

    for layer in range(LAYERS):
        at = pl.ds(layer * PLANE, PLANE)
        for s in range(4):
            walls_ref[s : s + 1, at] = 0.5 * jnp.sum(weights * states[s][layer], axis=0, keepdims=True)
        pbuf[layer] = jnp.sum(weights * states[4][layer], axis=0, keepdims=True) + 0.2 * chambers[3]
    pout_ref[...] = pbuf[cls]

    wait_sends(p_copy)
    wait_sends(part_copy)
    pltpu.make_async_copy(first31, first31, s_send.at[0]).wait()

    @pl.when(is_edge)
    def _():
        pltpu.make_async_copy(first32, first32, s_send.at[1]).wait()
        pltpu.make_async_copy(first32, first32, s_send.at[2]).wait()


def finish_kernel(m_ref, walls_ref, vec_ref, p_ref, out_hbm, pout_ref, out_v, sem):
    pout_ref[...] = p_ref[...]
    walls = [
        [jnp.broadcast_to(walls_ref[s : s + 1, i * 128 : (i + 1) * 128], (KC, 128)) for i in range(CHUNKS)]
        for s in range(4)
    ]
    copies = []
    step = NODES // GROUPS
    for g in range(GROUPS):
        for j in range(g * step, (g + 1) * step):
            at = pl.ds(j * KC, KC)
            v = [vec_ref[s, at, :] for s in range(4)]
            for i in range(CHUNKS):
                y = m_ref[i, at, :]
                for s in range(4):
                    y = y + v[s] * walls[s][i]
                out_v[at, pl.ds(i * 128, 128)] = y
        rows = pl.ds(g * step * KC, step * KC)
        copies.append(pltpu.make_async_copy(out_v.at[rows], out_hbm.at[rows], sem.at[g]))
        copies[-1].start()
    for copy in copies:
        copy.wait()


def shards(melt, counts, pressure, propagator, coupling, flux_weights):
    vmem = pl.BlockSpec(memory_space=pltpu.VMEM)
    hbm = pl.BlockSpec(memory_space=pltpu.HBM)
    dma = pltpu.SemaphoreType.DMA
    m, walls, vec, pout = pl.pallas_call(
        main_kernel,
        name="block_step",
        out_shape=(
            jax.ShapeDtypeStruct((CHUNKS, NODES * KC, 128), F32),
            jax.ShapeDtypeStruct((4, BLOCK), F32),
            jax.ShapeDtypeStruct((4, NODES * KC, 128), F32),
            jax.ShapeDtypeStruct((1, PLANE), F32),
        ),
        in_specs=[hbm] * 6,
        out_specs=(vmem, vmem, vmem, vmem),
        scratch_shapes=[
            pltpu.VMEM((CHUNKS, NODES * KC, 128), F32),
            pltpu.VMEM((KC * NODES, BLOCK), BF16),
            pltpu.VMEM((KC, BLOCK), jnp.int32),
            pltpu.VMEM((KC * NODES, NODES), F32),
            pltpu.VMEM((KC, NODES), F32),
            pltpu.VMEM((KC, NODES), F32),
            pltpu.VMEM((3, 4, KC, BLOCK), F32),
            pltpu.VMEM((3, 4, 1, PLANE), F32),
            pltpu.VMEM((64, 1, 128), F32),
            pltpu.VMEM((1, 1, 128), F32),
            pltpu.VMEM((LAYERS, 1, PLANE), F32),
            dma((CHUNKS,)), dma((5,)),
            dma((3, 4, 3)), dma((3, 4, 3)), dma((3, 4)), dma((3, 4)),
            dma((3,)), dma((2,)), pltpu.SemaphoreType.REGULAR,
        ],
        compiler_params=pltpu.CompilerParams(collective_id=0, has_side_effects=True, vmem_limit_bytes=32 << 20),
    )(
        *(
            pltpu.with_memory_space_constraint(x, pltpu.HBM)
            for x in (
                melt.reshape(NODES * KC, BLOCK), counts, pressure,
                propagator.reshape(CLASSES * NODES, NODES), coupling, flux_weights,
            )
        )
    )
    shells, pout = pl.pallas_call(
        finish_kernel,
        name="walls_into_shells",
        out_shape=(
            jax.ShapeDtypeStruct((NODES * KC, BLOCK), F32),
            jax.ShapeDtypeStruct((1, PLANE), F32),
        ),
        in_specs=[vmem, vmem, vmem, vmem],
        out_specs=(hbm, vmem),
        scratch_shapes=[pltpu.VMEM((NODES * KC, BLOCK), F32), dma((GROUPS,))],
        compiler_params=pltpu.CompilerParams(vmem_limit_bytes=32 << 20),
    )(m, walls, vec, pout)
    return shells.reshape(NODES, KC, BLOCK), pout


def solution(mesh):
    placed = (P(None, "cls", "cell"), P("cls", "cell"), P(("cell", "cls"), None), P(), P(), P())
    return jax.shard_map(
        shards,
        mesh=mesh,
        in_specs=placed,
        out_specs=(P(None, "cls", "cell"), P(("cell", "cls"), None)),
        check_vma=False,
    )
```

```python
import functools

import jax
import jax.numpy as jnp
from jax import lax
from jax.experimental import pallas as pl
from jax.experimental.pallas import tpu as pltpu
from jax.sharding import PartitionSpec as P

MESH = pl.DeviceIdType.MESH
F32 = jnp.float32
BF16 = jnp.bfloat16
NODES = 64
CLASSES = 32
SIDE = 16
PLANE = 256
LAYERS = 4
BLOCK = LAYERS * PLANE
KC = 8
NCELLS = 65536
COUNT_SCALE = 400.0
CHUNKS = 8
GROUPS = 8
FIRST = 5


HALO = tuple((r, d) for d, n in ((1, 6), (2, 4), (3, 2)) for r in range(n))
HALO_ROWS = len(HALO) + 1
OWN_ROWS = 8 * LAYERS + 1


def split2(x):
    hi = x.astype(BF16)
    return hi, (x - hi.astype(F32)).astype(BF16)


def dot_nn(a, b):
    return jnp.dot(a, b, preferred_element_type=F32)


def dot3(a, b):
    (ah, al), (bh, bl) = a, b
    return dot_nn(ah, bh) + (dot_nn(al, bh) + dot_nn(ah, bl))


def main_kernel(
    melt_hbm, counts_hbm, pres_ref, prop_hbm, coup_hbm, fw_hbm,
    m_ref, walls_ref, vec_ref, pout_ref,
    melt_v, counts_ref, prop_v, coup_v, fw_v, own, halo, halo_out, acc, srow, pbuf,
    load_sem, small_sem, own_send, own_recv, halo_send, halo_recv, s_send, s_recv, ready,
):
    cell = lax.axis_index("cell")
    cls = lax.axis_index("cls")
    core = cell % 2
    yy = (cell // 2) % 4
    zh = (cell // 8) % 2
    xx = cell // 16
    has_prev = cell > 0
    has_next = cell < 63

    loads = [
        pltpu.make_async_copy(melt_hbm.at[:, pl.ds(i * 128, 128)], melt_v.at[i], load_sem.at[i])
        for i in range(CHUNKS)
    ]
    smalls = [
        pltpu.make_async_copy(prop_hbm.at[pl.ds(cls * 512, 512)], prop_v, small_sem.at[0]),
        pltpu.make_async_copy(coup_hbm.at[pl.ds(cls * 8, 8)], coup_v, small_sem.at[1]),
        pltpu.make_async_copy(fw_hbm.at[pl.ds(cls * 8, 8)], fw_v, small_sem.at[2]),
        pltpu.make_async_copy(counts_hbm, counts_ref, small_sem.at[3]),
        pltpu.make_async_copy(pres_ref, own.at[cls, OWN_ROWS - 1], small_sem.at[4]),
        pltpu.make_async_copy(pres_ref, halo_out.at[0, HALO_ROWS - 1], small_sem.at[5]),
        pltpu.make_async_copy(pres_ref, halo_out.at[1, HALO_ROWS - 1], small_sem.at[6]),
    ]
    for copy in smalls + loads:
        copy.start()

    barrier = pltpu.get_barrier_semaphore()

    def signal(c, k):
        pl.semaphore_signal(barrier, inc=1, device_id=(c, k), device_id_type=MESH)

    def block_at(x, z, y, c):
        return ((x * 2 + z) * 4 + y) * 2 + c

    adds = jnp.logical_or(cls == 0, cls == 3)
    second = jnp.where(cls == 0, 1, 2)
    near = jnp.where(cls < 2, 3, 0)
    near2 = jnp.where(cls == 3, 1, 2)
    server = jnp.where(cls < 2, 0, 3)
    one = jnp.int32(1)

    @pl.when(has_prev)
    def _():
        for k in range(4):
            signal(cell - 1, k)

    @pl.when(has_next)
    def _():
        for k in range(4):
            signal(cell + 1, k)

    for d in range(4):
        signal(block_at((xx + d) % 4, 1 - zh, yy, core), near)
    for d in range(1, 4):
        signal(cell, (cls + d) % 4)
    for d in range(1, 4):
        signal(block_at((xx + d) % 4, zh, yy, core), server)
    for d in range(1, 8):
        signal((cell // 8) * 8 + (cell + d) % 8, cls)

    @pl.when(adds)
    def _():
        for d in range(4):
            signal(block_at((xx + d) % 4, 1 - zh, yy, core), near2)
        for d in range(1, 4):
            signal(block_at((xx + d) % 4, zh, yy, core), second)

    greeted = 17 + 7 * jnp.where(adds, one, 0) + 4 * jnp.where(has_prev, one, 0) + 4 * jnp.where(has_next, one, 0)

    def own_copy(k):
        return pltpu.make_async_remote_copy(
            src_ref=own.at[cls], dst_ref=own.at[cls], send_sem=own_send.at[k], recv_sem=own_recv.at[cls],
            device_id=(cell, k), device_id_type=MESH)

    def halo_copy(side, k):
        return pltpu.make_async_remote_copy(
            src_ref=halo_out.at[side], dst_ref=halo.at[1 - side, cls], send_sem=halo_send.at[side, k],
            recv_sem=halo_recv.at[1 - side, cls], device_id=(cell + (2 * side - 1), k), device_id_type=MESH)

    def each_copy(order, act):
        for classes in order:
            for k in classes:
                @pl.when(cls != k)
                def _(k=k):
                    act(own_copy(k))

            @pl.when(has_prev)
            def _(classes=classes):
                for k in classes:
                    act(halo_copy(0, k))

            @pl.when(has_next)
            def _(classes=classes):
                for k in classes:
                    act(halo_copy(1, k))

    @pl.when(jnp.logical_not(has_prev))
    def _():
        halo[0] = jnp.zeros((4, HALO_ROWS, 1, PLANE), F32)

    @pl.when(jnp.logical_not(has_next))
    def _():
        halo[1] = jnp.zeros((4, HALO_ROWS, 1, PLANE), F32)

    for copy in smalls:
        copy.wait()
    prop = prop_v[...]
    p_hi, p_lo = split2(prop)
    pp = jnp.concatenate([p_hi, p_lo], axis=1)
    lane = lax.broadcasted_iota(jnp.int32, (KC, 128), 1)
    row = lax.broadcasted_iota(jnp.int32, (KC, 128), 0)
    half = jnp.where(lane >= 64, 1, 0)

    def doubled(x):
        return jnp.concatenate([x, x], axis=1)

    def kron(x):
        return jnp.concatenate([jnp.where(row == 2 * v + half, x, 0.0) for v in range(4)], axis=1)

    def spread(r):
        return jnp.concatenate(split2(kron(r)), axis=0)

    def row_step(wide):
        y = dot_nn(wide, pp)
        y = y[:KC] + y[KC:]
        return y + pltpu.roll(y, 64, 1)

    fw = fw_v[...]
    coup = coup_v[...]
    wide_lane = lax.broadcasted_iota(jnp.int32, (NODES, NODES * KC), 1)
    wide_row = lax.broadcasted_iota(jnp.int32, (NODES, NODES * KC), 0)
    repeat8 = jnp.where(wide_lane // KC == wide_row, 1.0, 0.0).astype(BF16)
    own_class = (wide_lane % KC == wide_row % KC)[: 2 * KC]

    def flux_rows(r):
        both = jnp.concatenate(split2(r[:, :NODES]), axis=0)
        return jnp.where(own_class, dot_nn(both, repeat8), 0.0).astype(BF16)

    rs = [doubled(fw)]
    flux_w = []
    for t in range(4):
        rs.append(row_step(spread(rs[-1])))
        flux_w.append(flux_rows(rs[-1]))
    weights_f = jnp.concatenate(flux_w, axis=0)

    counts_f = counts_ref[...].astype(F32)
    flux = [[] for _ in range(4)]
    for n in range(CHUNKS // 2):
        loads[2 * n].wait()
        loads[2 * n + 1].wait()
        pair = jnp.concatenate([melt_v[2 * n], melt_v[2 * n + 1]], axis=1)
        y = dot_nn(weights_f, pair.astype(BF16))
        for t in range(4):
            flux[t].append(y[16 * t : 16 * t + 8] + y[16 * t + 8 : 16 * t + 16])
    scale = 1.0 / (COUNT_SCALE * CLASSES)

    def put(r, value):
        for l in range(LAYERS):
            tile = value[:, l * PLANE : (l + 1) * PLANE]
            own[cls, r * LAYERS + l] = tile
            if (r, l + 1) in HALO:
                halo_out[0, HALO.index((r, l + 1))] = tile
            if (r, LAYERS - l) in HALO:
                halo_out[1, HALO.index((r, LAYERS - l))] = tile

    for t in range(4):
        a_t = jnp.sum(rs[t][:, :NODES] * coup, axis=1, keepdims=True)
        put(2 * t + 1, jnp.sum(counts_f * a_t, axis=0, keepdims=True) * scale)
    for t in range(4):
        put(2 * t, jnp.sum(counts_f * jnp.concatenate(flux[t], axis=1), axis=0, keepdims=True) * scale)

    pl.semaphore_wait(barrier, greeted)
    each_copy(((0, 3), (1, 2)), lambda copy: copy.start())

    def announce(c, k):
        pl.semaphore_signal(ready, inc=1, device_id=(c, k), device_id_type=MESH)

    for d in range(1, 4):
        announce(block_at((xx + d) % 4, zh, yy, core), server)
    for d in range(4):
        announce(block_at((xx + d) % 4, 1 - zh, yy, core), near)

    @pl.when(jnp.logical_not(adds))
    def _():
        announce(cell, server)

    def col_step(v):
        hi, lo = split2(v[:, :NODES])
        lhs = jnp.concatenate([hi, lo], axis=0)
        nt = (((1,), (1,)), ((), ()))
        y = lax.dot_general(lhs, p_hi, nt, preferred_element_type=F32)
        y = y[:KC] + y[KC:] + lax.dot_general(hi, p_lo, nt, preferred_element_type=F32)
        z = jnp.zeros((KC, 128), F32)
        for q in range(4):
            z = z + jnp.where(row == 2 * q + half, y[:, 128 * q : 128 * (q + 1)], 0.0)
        return z + pltpu.roll(z, 64, 1)

    vs = [doubled(coup)]
    for s in range(3):
        vs.append(col_step(vs[-1]))
    for s in range(4):
        for j in range(NODES):
            vec_ref[s, pl.ds(j * KC, KC), :] = jnp.broadcast_to(vs[3 - s][:, j : j + 1], (KC, 128))

    def powers_into_melt(classes):
        for k in classes:
            base = split2(prop_v[pl.ds(k * NODES, NODES), :])
            two = split2(dot3(base, base))
            four_hi, four_lo = split2(dot3(two, two))
            lhs = jnp.concatenate([four_hi, four_hi, four_lo], axis=1)
            at = pl.ds(k, NODES, stride=KC)
            for n in range(CHUNKS // 2):
                x = jnp.concatenate([melt_v[2 * n, at, :], melt_v[2 * n + 1, at, :]], axis=1)
                x_hi, x_lo = split2(x)
                y = dot_nn(lhs, jnp.concatenate([x_hi, x_lo, x_hi], axis=0))
                m_ref[2 * n, at, :] = y[:, :128]
                m_ref[2 * n + 1, at, :] = y[:, 128:]

    powers_into_melt(range(0, FIRST))

    for d in range(1, 4):
        k = (cls + d) % 4
        pltpu.make_async_copy(own.at[k], own.at[k], own_recv.at[k]).wait()
    for side, there in ((0, has_prev), (1, has_next)):
        @pl.when(there)
        def _(side=side):
            for k in range(4):
                pltpu.make_async_copy(halo.at[side, k], halo.at[side, k], halo_recv.at[side, k]).wait()

    inside = [jnp.where(has_prev, 1.0, 0.0).astype(F32), None, jnp.where(has_next, 1.0, 0.0).astype(F32)]

    lane2 = lax.broadcasted_iota(jnp.int32, (KC, PLANE), 1)
    row2 = lax.broadcasted_iota(jnp.int32, (KC, PLANE), 0)

    def field(layer, r):
        if 0 <= layer < LAYERS:
            rows = [own[k, r * LAYERS + layer] for k in range(4)]
        else:
            side, d = (0, -layer) if layer < 0 else (1, layer - LAYERS + 1)
            rows = [halo[side, k, HALO.index((r, d))] for k in range(4)]
        return jnp.broadcast_to(rows[0] + rows[1] + (rows[2] + rows[3]), (KC, PLANE))

    def start_pressure(layer):
        if 0 <= layer < LAYERS:
            return own[layer, OWN_ROWS - 1]
        return halo[0, layer + 4, HALO_ROWS - 1] if layer < 0 else halo[1, layer - LAYERS, HALO_ROWS - 1]

    def plane_neighbours(x):
        west = jnp.where(lane2 % SIDE == 0, 0.0, pltpu.roll(x, 1, 1))
        east = jnp.where(lane2 % SIDE == SIDE - 1, 0.0, pltpu.roll(x, PLANE - 1, 1))
        north = jnp.where(lane2 < SIDE, 0.0, pltpu.roll(x, SIDE, 1))
        south = jnp.where(lane2 >= PLANE - SIDE, 0.0, pltpu.roll(x, PLANE - SIDE, 1))
        return west + east + (north + south)

    states = [{}]
    for layer in range(-4, 8):
        states[0][layer] = jnp.where(row2 == 0, jnp.broadcast_to(start_pressure(layer), (KC, PLANE)), 0.0)
    gases = []
    fields = {}

    def field_of(layer, r):
        if (layer, r) not in fields:
            fields[layer, r] = field(layer, r)
        return fields[layer, r]

    for s in range(4):
        gas = {}
        reach = 3 - s
        for layer in range(-reach, LAYERS + reach):
            g = jnp.where(row2 == 0, field_of(layer, 2 * s), 0.0)
            for m in range(s + 1):
                g = g + field_of(layer, 2 * m + 1) * (0.5 * states[s - m][layer])
            gas[layer] = g
        gases.append(gas)
        new = {}
        for layer in range(-reach, LAYERS + reach):
            x = states[s][layer]
            around = plane_neighbours(x) + (states[s][layer - 1] + states[s][layer + 1])
            x = x + 0.15 * (around - 6.0 * x) + 0.1 * gas[layer] - 0.2 * x
            x = x + jnp.where(row2 == s + 1, 0.2, 0.0)
            if layer < 0:
                x = x * inside[0]
            if layer >= LAYERS:
                x = x * inside[2]
            new[layer] = x
        states.append(new)

    packed = jnp.zeros((KC, 128), F32)
    for s in range(4):
        t = gases[s][0] + gases[s][1] + (gases[s][2] + gases[s][3])
        t = jnp.sum(t[:, :128] + t[:, 128:], axis=1, keepdims=True)
        packed = packed + jnp.where(jnp.logical_and(lane == s * 4 + row, row < 4), t, 0.0)
    packed = jnp.sum(packed, axis=0, keepdims=True)
    slot = (xx * 4 + yy) * 2 + core
    srow[0] = packed
    acc[zh * 32 + slot] = packed

    hops = [0, 1, 2, 1]
    offsets = sorted(
        ((dx, dy, dc) for dx in range(4) for dy in range(4) for dc in range(2)),
        key=lambda o: -(hops[o[0]] + hops[o[1]] + 0.3 * o[2]),
    )

    def block_of(o, z):
        return block_at((xx + o[0]) % 4, z, (yy + o[1]) % 4, (core + o[2]) % 2)

    def sum_copy(c, k, sem, arrived):
        return pltpu.make_async_remote_copy(
            src_ref=srow.at[0], dst_ref=acc.at[zh * 32 + slot], send_sem=sem, recv_sem=arrived,
            device_id=(c, k), device_id_type=MESH)

    @pl.when(adds)
    def _():
        pl.semaphore_wait(ready, 15)
        for o in offsets:
            sum_copy(block_of(o, 1 - zh), near2, s_send.at[2], s_recv.at[1]).start()
            sum_copy(block_of(o, 1 - zh), near, s_send.at[1], s_recv.at[1]).start()
            if o != (0, 0, 0):
                sum_copy(block_of(o, zh), second, s_send.at[3], s_recv.at[0]).start()
                sum_copy(block_of(o, zh), cls, s_send.at[0], s_recv.at[0]).start()

    powers_into_melt(range(FIRST, KC))
    first31 = acc.at[pl.ds(0, 31)]
    first32 = acc.at[pl.ds(0, 32)]
    pltpu.make_async_copy(first31, first31, s_recv.at[0]).wait()
    pltpu.make_async_copy(first32, first32, s_recv.at[1]).wait()
    total = jnp.sum(acc[...], axis=0)

    def coefficient(s, r):
        return total[:, s * 4 + r : s * 4 + r + 1]

    chambers = []
    for s in range(4):
        t = coefficient(s, 0)
        for r in range(s):
            t = t + chambers[r] * coefficient(s, r + 1)
        chambers.append(1.5 - 0.5 * (t / NCELLS))
    weights = jnp.where(row2 == 0, 1.0, 0.0)
    for r in range(3):
        weights = jnp.where(row2 == r + 1, chambers[r], weights)

    for layer in range(LAYERS):
        at = pl.ds(layer * PLANE, PLANE)
        for s in range(4):
            walls_ref[s : s + 1, at] = 0.5 * jnp.sum(weights * states[s][layer], axis=0, keepdims=True)
        pbuf[layer] = jnp.sum(weights * states[4][layer], axis=0, keepdims=True) + 0.2 * chambers[3]
    pout_ref[...] = pbuf[cls]

    each_copy(((0, 3), (1, 2)), lambda copy: copy.wait_send())

    @pl.when(adds)
    def _():
        pltpu.make_async_copy(first31, first31, s_send.at[0]).wait()
        pltpu.make_async_copy(first32, first32, s_send.at[1]).wait()
        pltpu.make_async_copy(first32, first32, s_send.at[2]).wait()
        pltpu.make_async_copy(first31, first31, s_send.at[3]).wait()


def finish_kernel(m_ref, walls_ref, vec_ref, p_ref, out_hbm, pout_hbm, out_v, sem):
    p_out = pltpu.make_async_copy(p_ref, pout_hbm, sem.at[GROUPS])
    p_out.start()
    walls = [
        [jnp.broadcast_to(walls_ref[s : s + 1, i * 128 : (i + 1) * 128], (KC, 128)) for i in range(CHUNKS)]
        for s in range(4)
    ]
    copies = [p_out]
    step = NODES // GROUPS
    for g in range(GROUPS):
        for j in range(g * step, (g + 1) * step):
            at = pl.ds(j * KC, KC)
            v = [vec_ref[s, at, :] for s in range(4)]
            for i in range(CHUNKS):
                y = m_ref[i, at, :]
                for s in range(4):
                    y = y + v[s] * walls[s][i]
                out_v[at, pl.ds(i * 128, 128)] = y
        rows = pl.ds(g * step * KC, step * KC)
        copies.append(pltpu.make_async_copy(out_v.at[rows], out_hbm.at[rows], sem.at[g]))
        copies[-1].start()
    for copy in copies:
        copy.wait()


def shards(melt, counts, pressure, propagator, coupling, flux_weights):
    vmem = pl.BlockSpec(memory_space=pltpu.VMEM)
    hbm = pl.BlockSpec(memory_space=pltpu.HBM)
    dma = pltpu.SemaphoreType.DMA
    m, walls, vec, pout = pl.pallas_call(
        main_kernel,
        name="block_step",
        out_shape=(
            jax.ShapeDtypeStruct((CHUNKS, NODES * KC, 128), F32),
            jax.ShapeDtypeStruct((4, BLOCK), F32),
            jax.ShapeDtypeStruct((4, NODES * KC, 128), F32),
            jax.ShapeDtypeStruct((1, PLANE), F32),
        ),
        in_specs=[hbm] * 6,
        out_specs=(vmem, vmem, vmem, vmem),
        scratch_shapes=[
            pltpu.VMEM((CHUNKS, NODES * KC, 128), F32),
            pltpu.VMEM((KC, BLOCK), jnp.int32),
            pltpu.VMEM((KC * NODES, NODES), F32),
            pltpu.VMEM((KC, NODES), F32),
            pltpu.VMEM((KC, NODES), F32),
            pltpu.VMEM((4, OWN_ROWS, 1, PLANE), F32),
            pltpu.VMEM((2, 4, HALO_ROWS, 1, PLANE), F32),
            pltpu.VMEM((2, HALO_ROWS, 1, PLANE), F32),
            pltpu.VMEM((64, 1, 128), F32),
            pltpu.VMEM((1, 1, 128), F32),
            pltpu.VMEM((LAYERS, 1, PLANE), F32),
            dma((CHUNKS,)), dma((7,)),
            dma((4,)), dma((4,)), dma((2, 4)), dma((2, 4)),
            dma((4,)), dma((2,)), pltpu.SemaphoreType.REGULAR,
        ],
        compiler_params=pltpu.CompilerParams(collective_id=0, has_side_effects=True, vmem_limit_bytes=32 << 20),
    )(
        *(
            pltpu.with_memory_space_constraint(x, pltpu.HBM)
            for x in (
                melt.reshape(NODES * KC, BLOCK), counts, pressure,
                propagator.reshape(CLASSES * NODES, NODES), coupling, flux_weights,
            )
        )
    )
    shells, pout = pl.pallas_call(
        finish_kernel,
        name="walls_into_shells",
        out_shape=(
            jax.ShapeDtypeStruct((NODES * KC, BLOCK), F32),
            jax.ShapeDtypeStruct((1, PLANE), F32),
        ),
        in_specs=[vmem, vmem, vmem, vmem],
        out_specs=(hbm, hbm),
        scratch_shapes=[pltpu.VMEM((NODES * KC, BLOCK), F32), dma((GROUPS + 1,))],
        compiler_params=pltpu.CompilerParams(vmem_limit_bytes=32 << 20),
    )(m, walls, vec, pout)
    return shells.reshape(NODES, KC, BLOCK), pout


def solution(mesh):
    placed = (P(None, "cls", "cell"), P("cls", "cell"), P(("cell", "cls"), None), P(), P(), P())
    return jax.shard_map(
        shards,
        mesh=mesh,
        in_specs=placed,
        out_specs=(P(None, "cls", "cell"), P(("cell", "cls"), None)),
        check_vma=False,
    )
```

```python
import functools

import jax
import jax.numpy as jnp
from jax import lax
from jax.experimental import pallas as pl
from jax.experimental.pallas import tpu as pltpu
from jax.sharding import PartitionSpec as P

MESH = pl.DeviceIdType.MESH
F32 = jnp.float32
BF16 = jnp.bfloat16
NODES = 64
CLASSES = 32
SIDE = 16
PLANE = 256
LAYERS = 4
BLOCK = LAYERS * PLANE
KC = 8
NCELLS = 65536
COUNT_SCALE = 400.0
CHUNKS = 8
GROUPS = 8
FIRST = 7


HALO = tuple((r, d) for d, n in ((1, 6), (2, 4), (3, 2)) for r in range(n))
HALO_ROWS = len(HALO) + 1
OWN_ROWS = 8 * LAYERS + 1


def split2(x):
    hi = x.astype(BF16)
    return hi, (x - hi.astype(F32)).astype(BF16)


def dot_nn(a, b):
    return jnp.dot(a, b, preferred_element_type=F32)


def dot3(a, b):
    (ah, al), (bh, bl) = a, b
    return dot_nn(ah, bh) + (dot_nn(al, bh) + dot_nn(ah, bl))


def main_kernel(
    melt_hbm, counts_hbm, pres_ref, prop_hbm, coup_hbm, fw_hbm,
    m_ref, walls_ref, vec_ref, pout_ref,
    melt_v, counts_ref, prop_v, coup_v, fw_v, own, halo, halo_out, acc, srow, pbuf,
    load_sem, small_sem, own_send, own_recv, halo_send, halo_recv, s_send, s_recv, ready,
):
    cell = lax.axis_index("cell")
    cls = lax.axis_index("cls")
    core = lax.rem(cell, 2)
    yy = lax.rem(lax.div(cell, 2), 4)
    zh = lax.rem(lax.div(cell, 8), 2)
    xx = lax.div(cell, 16)
    has_prev = cell > 0
    has_next = cell < 63

    loads = [
        pltpu.make_async_copy(melt_hbm.at[:, pl.ds(i * 128, 128)], melt_v.at[i], load_sem.at[i])
        for i in range(CHUNKS)
    ]
    smalls = [
        pltpu.make_async_copy(prop_hbm.at[pl.ds(cls * 512, 512)], prop_v, small_sem.at[0]),
        pltpu.make_async_copy(coup_hbm.at[pl.ds(cls * 8, 8)], coup_v, small_sem.at[1]),
        pltpu.make_async_copy(fw_hbm.at[pl.ds(cls * 8, 8)], fw_v, small_sem.at[2]),
        pltpu.make_async_copy(counts_hbm, counts_ref, small_sem.at[3]),
        pltpu.make_async_copy(pres_ref, own.at[cls, OWN_ROWS - 1], small_sem.at[4]),
        pltpu.make_async_copy(pres_ref, halo_out.at[0, HALO_ROWS - 1], small_sem.at[5]),
        pltpu.make_async_copy(pres_ref, halo_out.at[1, HALO_ROWS - 1], small_sem.at[6]),
    ]
    for copy in smalls + loads:
        copy.start()

    barrier = pltpu.get_barrier_semaphore()

    def signal(c, k):
        pl.semaphore_signal(barrier, inc=1, device_id=(c, k), device_id_type=MESH)

    def block_at(x, z, y, c):
        return ((x * 2 + z) * 4 + y) * 2 + c

    adds = jnp.logical_or(cls == 0, cls == 3)
    second = jnp.where(cls == 0, 1, 2)
    near = jnp.where(cls < 2, 3, 0)
    near2 = jnp.where(cls == 3, 1, 2)
    server = jnp.where(cls < 2, 0, 3)
    one = jnp.int32(1)

    @pl.when(has_prev)
    def _():
        for k in range(4):
            signal(cell - 1, k)

    @pl.when(has_next)
    def _():
        for k in range(4):
            signal(cell + 1, k)

    for d in range(4):
        signal(block_at(lax.rem(xx + d, 4), 1 - zh, yy, core), near)
    for d in range(1, 4):
        signal(cell, lax.rem(cls + d, 4))
    for d in range(1, 4):
        signal(block_at(lax.rem(xx + d, 4), zh, yy, core), server)
    for d in range(1, 8):
        signal(lax.div(cell, 8) * 8 + lax.rem(cell + d, 8), cls)

    @pl.when(adds)
    def _():
        for d in range(4):
            signal(block_at(lax.rem(xx + d, 4), 1 - zh, yy, core), near2)
        for d in range(1, 4):
            signal(block_at(lax.rem(xx + d, 4), zh, yy, core), second)

    greeted = 17 + 7 * jnp.where(adds, one, 0) + 4 * jnp.where(has_prev, one, 0) + 4 * jnp.where(has_next, one, 0)

    def own_copy(k):
        return pltpu.make_async_remote_copy(
            src_ref=own.at[cls], dst_ref=own.at[cls], send_sem=own_send.at[k], recv_sem=own_recv.at[cls],
            device_id=(cell, k), device_id_type=MESH)

    def halo_copy(side, k):
        return pltpu.make_async_remote_copy(
            src_ref=halo_out.at[side], dst_ref=halo.at[1 - side, cls], send_sem=halo_send.at[side, k],
            recv_sem=halo_recv.at[1 - side, cls], device_id=(cell + (2 * side - 1), k), device_id_type=MESH)

    def each_copy(order, act):
        for classes in order:
            @pl.when(has_prev)
            def _(classes=classes):
                for k in classes:
                    act(halo_copy(0, k))

            @pl.when(has_next)
            def _(classes=classes):
                for k in classes:
                    act(halo_copy(1, k))

            for k in classes:
                @pl.when(cls != k)
                def _(k=k):
                    act(own_copy(k))

    @pl.when(jnp.logical_not(has_prev))
    def _():
        halo[0] = jnp.zeros((4, HALO_ROWS, 1, PLANE), F32)

    @pl.when(jnp.logical_not(has_next))
    def _():
        halo[1] = jnp.zeros((4, HALO_ROWS, 1, PLANE), F32)

    for copy in smalls:
        copy.wait()
    prop = prop_v[...]
    p_hi, p_lo = split2(prop)
    pp = jnp.concatenate([p_hi, p_lo], axis=1)
    lane = lax.broadcasted_iota(jnp.int32, (KC, 128), 1)
    row = lax.broadcasted_iota(jnp.int32, (KC, 128), 0)
    half = jnp.where(lane >= 64, 1, 0)

    def doubled(x):
        return jnp.concatenate([x, x], axis=1)

    def kron(x):
        return jnp.concatenate([jnp.where(row == 2 * v + half, x, 0.0) for v in range(4)], axis=1)

    def spread(r):
        return jnp.concatenate(split2(kron(r)), axis=0)

    def row_step(wide):
        y = dot_nn(wide, pp)
        y = y[:KC] + y[KC:]
        return y + pltpu.roll(y, 64, 1)

    fw = fw_v[...]
    coup = coup_v[...]
    wide_lane = lax.broadcasted_iota(jnp.int32, (NODES, NODES * KC), 1)
    wide_row = lax.broadcasted_iota(jnp.int32, (NODES, NODES * KC), 0)
    repeat8 = jnp.where(wide_lane // KC == wide_row, 1.0, 0.0).astype(BF16)
    own_class = (wide_lane % KC == wide_row % KC)[: 2 * KC]

    def flux_rows(r):
        both = jnp.concatenate(split2(r[:, :NODES]), axis=0)
        return jnp.where(own_class, dot_nn(both, repeat8), 0.0).astype(BF16)

    rs = [doubled(fw)]
    flux_w = []
    for t in range(4):
        rs.append(row_step(spread(rs[-1])))
        flux_w.append(flux_rows(rs[-1]))
    weights_f = jnp.concatenate(flux_w, axis=0)

    counts_f = counts_ref[...].astype(F32)
    flux = [[] for _ in range(4)]
    for n in range(CHUNKS // 2):
        loads[2 * n].wait()
        loads[2 * n + 1].wait()
        pair = jnp.concatenate([melt_v[2 * n], melt_v[2 * n + 1]], axis=1)
        y = dot_nn(weights_f, pair.astype(BF16))
        for t in range(4):
            flux[t].append(y[16 * t : 16 * t + 8] + y[16 * t + 8 : 16 * t + 16])
    scale = 1.0 / (COUNT_SCALE * CLASSES)

    def put(r, value):
        for l in range(LAYERS):
            tile = value[:, l * PLANE : (l + 1) * PLANE]
            own[cls, r * LAYERS + l] = tile
            if (r, l + 1) in HALO:
                halo_out[0, HALO.index((r, l + 1))] = tile
            if (r, LAYERS - l) in HALO:
                halo_out[1, HALO.index((r, LAYERS - l))] = tile

    for t in range(4):
        a_t = jnp.sum(rs[t][:, :NODES] * coup, axis=1, keepdims=True)
        put(2 * t + 1, jnp.sum(counts_f * a_t, axis=0, keepdims=True) * scale)
    for t in range(4):
        put(2 * t, jnp.sum(counts_f * jnp.concatenate(flux[t], axis=1), axis=0, keepdims=True) * scale)

    pl.semaphore_wait(barrier, greeted)
    each_copy(((0, 3),), lambda copy: copy.start())

    def announce(c, k):
        pl.semaphore_signal(ready, inc=1, device_id=(c, k), device_id_type=MESH)

    for d in range(1, 4):
        announce(block_at(lax.rem(xx + d, 4), zh, yy, core), server)
    for d in range(4):
        announce(block_at(lax.rem(xx + d, 4), 1 - zh, yy, core), near)

    @pl.when(jnp.logical_not(adds))
    def _():
        announce(cell, server)

    def col_step(v):
        hi, lo = split2(v[:, :NODES])
        lhs = jnp.concatenate([hi, lo], axis=0)
        nt = (((1,), (1,)), ((), ()))
        y = lax.dot_general(lhs, p_hi, nt, preferred_element_type=F32)
        y = y[:KC] + y[KC:] + lax.dot_general(hi, p_lo, nt, preferred_element_type=F32)
        z = jnp.zeros((KC, 128), F32)
        for q in range(4):
            z = z + jnp.where(row == 2 * q + half, y[:, 128 * q : 128 * (q + 1)], 0.0)
        return z + pltpu.roll(z, 64, 1)

    vs = [doubled(coup)]
    for s in range(3):
        vs.append(col_step(vs[-1]))
    for s in range(4):
        for j in range(NODES):
            vec_ref[s, pl.ds(j * KC, KC), :] = jnp.broadcast_to(vs[3 - s][:, j : j + 1], (KC, 128))

    def powers_into_melt(classes):
        for k in classes:
            base = split2(prop_v[pl.ds(k * NODES, NODES), :])
            two = split2(dot3(base, base))
            four_hi, four_lo = split2(dot3(two, two))
            lhs = jnp.concatenate([four_hi, four_hi, four_lo], axis=1)
            at = pl.ds(k, NODES, stride=KC)
            for n in range(CHUNKS // 2):
                x = jnp.concatenate([melt_v[2 * n, at, :], melt_v[2 * n + 1, at, :]], axis=1)
                x_hi, x_lo = split2(x)
                y = dot_nn(lhs, jnp.concatenate([x_hi, x_lo, x_hi], axis=0))
                m_ref[2 * n, at, :] = y[:, :128]
                m_ref[2 * n + 1, at, :] = y[:, 128:]

    powers_into_melt(range(0, 3))
    each_copy(((1, 2),), lambda copy: copy.start())
    powers_into_melt(range(3, FIRST))

    for d in range(1, 4):
        k = lax.rem(cls + d, 4)
        pltpu.make_async_copy(own.at[k], own.at[k], own_recv.at[k]).wait()
    for side, there in ((0, has_prev), (1, has_next)):
        @pl.when(there)
        def _(side=side):
            for k in range(4):
                pltpu.make_async_copy(halo.at[side, k], halo.at[side, k], halo_recv.at[side, k]).wait()

    inside = [jnp.where(has_prev, 1.0, 0.0).astype(F32), None, jnp.where(has_next, 1.0, 0.0).astype(F32)]

    lane2 = lax.broadcasted_iota(jnp.int32, (KC, PLANE), 1)
    row2 = lax.broadcasted_iota(jnp.int32, (KC, PLANE), 0)

    def field(layer, r):
        if 0 <= layer < LAYERS:
            rows = [own[k, r * LAYERS + layer] for k in range(4)]
        else:
            side, d = (0, -layer) if layer < 0 else (1, layer - LAYERS + 1)
            rows = [halo[side, k, HALO.index((r, d))] for k in range(4)]
        return jnp.broadcast_to(rows[0] + rows[1] + (rows[2] + rows[3]), (KC, PLANE))

    def start_pressure(layer):
        if 0 <= layer < LAYERS:
            return own[layer, OWN_ROWS - 1]
        return halo[0, layer + 4, HALO_ROWS - 1] if layer < 0 else halo[1, layer - LAYERS, HALO_ROWS - 1]

    def plane_neighbours(x):
        west = jnp.where(lane2 % SIDE == 0, 0.0, pltpu.roll(x, 1, 1))
        east = jnp.where(lane2 % SIDE == SIDE - 1, 0.0, pltpu.roll(x, PLANE - 1, 1))
        north = jnp.where(lane2 < SIDE, 0.0, pltpu.roll(x, SIDE, 1))
        south = jnp.where(lane2 >= PLANE - SIDE, 0.0, pltpu.roll(x, PLANE - SIDE, 1))
        return west + east + (north + south)

    states = [{}]
    for layer in range(-4, 8):
        states[0][layer] = jnp.where(row2 == 0, jnp.broadcast_to(start_pressure(layer), (KC, PLANE)), 0.0)
    gases = []
    fields = {}

    def field_of(layer, r):
        if (layer, r) not in fields:
            fields[layer, r] = field(layer, r)
        return fields[layer, r]

    for s in range(4):
        gas = {}
        reach = 3 - s
        for layer in range(-reach, LAYERS + reach):
            g = jnp.where(row2 == 0, field_of(layer, 2 * s), 0.0)
            for m in range(s + 1):
                g = g + field_of(layer, 2 * m + 1) * (0.5 * states[s - m][layer])
            gas[layer] = g
        gases.append(gas)
        new = {}
        for layer in range(-reach, LAYERS + reach):
            x = states[s][layer]
            around = plane_neighbours(x) + (states[s][layer - 1] + states[s][layer + 1])
            x = x + 0.15 * (around - 6.0 * x) + 0.1 * gas[layer] - 0.2 * x
            x = x + jnp.where(row2 == s + 1, 0.2, 0.0)
            if layer < 0:
                x = x * inside[0]
            if layer >= LAYERS:
                x = x * inside[2]
            new[layer] = x
        states.append(new)

    packed = jnp.zeros((KC, 128), F32)
    for s in range(4):
        t = gases[s][0] + gases[s][1] + (gases[s][2] + gases[s][3])
        t = jnp.sum(t[:, :128] + t[:, 128:], axis=1, keepdims=True)
        packed = packed + jnp.where(jnp.logical_and(lane == s * 4 + row, row < 4), t, 0.0)
    packed = jnp.sum(packed, axis=0, keepdims=True)
    slot = (xx * 4 + yy) * 2 + core
    srow[0] = packed
    acc[zh * 32 + slot] = packed

    hops = [0, 1, 2, 1]
    offsets = sorted(
        ((dx, dy, dc) for dx in range(4) for dy in range(4) for dc in range(2)),
        key=lambda o: -(hops[o[0]] + hops[o[1]] + 0.3 * o[2]),
    )

    def block_of(o, z):
        return block_at(lax.rem(xx + o[0], 4), z, lax.rem(yy + o[1], 4), lax.rem(core + o[2], 2))

    def sum_copy(c, k, sem, arrived):
        return pltpu.make_async_remote_copy(
            src_ref=srow.at[0], dst_ref=acc.at[zh * 32 + slot], send_sem=sem, recv_sem=arrived,
            device_id=(c, k), device_id_type=MESH)

    @pl.when(adds)
    def _():
        pl.semaphore_wait(ready, 15)
        for o in offsets:
            sum_copy(block_of(o, 1 - zh), near2, s_send.at[2], s_recv.at[1]).start()
            sum_copy(block_of(o, 1 - zh), near, s_send.at[1], s_recv.at[1]).start()
            if o != (0, 0, 0):
                sum_copy(block_of(o, zh), second, s_send.at[3], s_recv.at[0]).start()
                sum_copy(block_of(o, zh), cls, s_send.at[0], s_recv.at[0]).start()

    powers_into_melt(range(FIRST, KC))
    first31 = acc.at[pl.ds(0, 31)]
    first32 = acc.at[pl.ds(0, 32)]
    pltpu.make_async_copy(first31, first31, s_recv.at[0]).wait()
    pltpu.make_async_copy(first32, first32, s_recv.at[1]).wait()
    total = jnp.sum(acc[...], axis=0)

    def coefficient(s, r):
        return total[:, s * 4 + r : s * 4 + r + 1]

    chambers = []
    for s in range(4):
        t = coefficient(s, 0)
        for r in range(s):
            t = t + chambers[r] * coefficient(s, r + 1)
        chambers.append(1.5 - 0.5 * (t / NCELLS))
    weights = jnp.where(row2 == 0, 1.0, 0.0)
    for r in range(3):
        weights = jnp.where(row2 == r + 1, chambers[r], weights)

    for layer in range(LAYERS):
        at = pl.ds(layer * PLANE, PLANE)
        for s in range(4):
            walls_ref[s : s + 1, at] = 0.5 * jnp.sum(weights * states[s][layer], axis=0, keepdims=True)
        pbuf[layer] = jnp.sum(weights * states[4][layer], axis=0, keepdims=True) + 0.2 * chambers[3]
    pout_ref[...] = pbuf[cls]

    each_copy(((0, 3), (1, 2)), lambda copy: copy.wait_send())

    @pl.when(adds)
    def _():
        pltpu.make_async_copy(first31, first31, s_send.at[0]).wait()
        pltpu.make_async_copy(first32, first32, s_send.at[1]).wait()
        pltpu.make_async_copy(first32, first32, s_send.at[2]).wait()
        pltpu.make_async_copy(first31, first31, s_send.at[3]).wait()


def finish_kernel(m_ref, walls_ref, vec_ref, p_ref, out_hbm, pout_hbm, out_v, sem):
    p_out = pltpu.make_async_copy(p_ref, pout_hbm, sem.at[GROUPS])
    p_out.start()
    walls = [
        [jnp.broadcast_to(walls_ref[s : s + 1, i * 128 : (i + 1) * 128], (KC, 128)) for i in range(CHUNKS)]
        for s in range(4)
    ]
    copies = [p_out]
    step = NODES // GROUPS
    for g in range(GROUPS):
        for j in range(g * step, (g + 1) * step):
            at = pl.ds(j * KC, KC)
            v = [vec_ref[s, at, :] for s in range(4)]
            for i in range(CHUNKS):
                y = m_ref[i, at, :]
                for s in range(4):
                    y = y + v[s] * walls[s][i]
                out_v[at, pl.ds(i * 128, 128)] = y
        rows = pl.ds(g * step * KC, step * KC)
        copies.append(pltpu.make_async_copy(out_v.at[rows], out_hbm.at[rows], sem.at[g]))
        copies[-1].start()
    for copy in copies:
        copy.wait()


def shards(melt, counts, pressure, propagator, coupling, flux_weights):
    vmem = pl.BlockSpec(memory_space=pltpu.VMEM)
    hbm = pl.BlockSpec(memory_space=pltpu.HBM)
    dma = pltpu.SemaphoreType.DMA
    m, walls, vec, pout = pl.pallas_call(
        main_kernel,
        name="block_step",
        out_shape=(
            jax.ShapeDtypeStruct((CHUNKS, NODES * KC, 128), F32),
            jax.ShapeDtypeStruct((4, BLOCK), F32),
            jax.ShapeDtypeStruct((4, NODES * KC, 128), F32),
            jax.ShapeDtypeStruct((1, PLANE), F32),
        ),
        in_specs=[hbm] * 6,
        out_specs=(vmem, vmem, vmem, vmem),
        scratch_shapes=[
            pltpu.VMEM((CHUNKS, NODES * KC, 128), F32),
            pltpu.VMEM((KC, BLOCK), jnp.int32),
            pltpu.VMEM((KC * NODES, NODES), F32),
            pltpu.VMEM((KC, NODES), F32),
            pltpu.VMEM((KC, NODES), F32),
            pltpu.VMEM((4, OWN_ROWS, 1, PLANE), F32),
            pltpu.VMEM((2, 4, HALO_ROWS, 1, PLANE), F32),
            pltpu.VMEM((2, HALO_ROWS, 1, PLANE), F32),
            pltpu.VMEM((64, 1, 128), F32),
            pltpu.VMEM((1, 1, 128), F32),
            pltpu.VMEM((LAYERS, 1, PLANE), F32),
            dma((CHUNKS,)), dma((7,)),
            dma((4,)), dma((4,)), dma((2, 4)), dma((2, 4)),
            dma((4,)), dma((2,)), pltpu.SemaphoreType.REGULAR,
        ],
        compiler_params=pltpu.CompilerParams(collective_id=0, has_side_effects=True, vmem_limit_bytes=32 << 20),
    )(
        *(
            pltpu.with_memory_space_constraint(x, pltpu.HBM)
            for x in (
                melt.reshape(NODES * KC, BLOCK), counts, pressure,
                propagator.reshape(CLASSES * NODES, NODES), coupling, flux_weights,
            )
        )
    )
    shells, pout = pl.pallas_call(
        finish_kernel,
        name="walls_into_shells",
        out_shape=(
            jax.ShapeDtypeStruct((NODES * KC, BLOCK), F32),
            jax.ShapeDtypeStruct((1, PLANE), F32),
        ),
        in_specs=[vmem, vmem, vmem, vmem],
        out_specs=(hbm, hbm),
        scratch_shapes=[pltpu.VMEM((NODES * KC, BLOCK), F32), dma((GROUPS + 1,))],
        compiler_params=pltpu.CompilerParams(vmem_limit_bytes=32 << 20),
    )(m, walls, vec, pout)
    return shells.reshape(NODES, KC, BLOCK), pout


def solution(mesh):
    placed = (P(None, "cls", "cell"), P("cls", "cell"), P(("cell", "cls"), None), P(), P(), P())
    return jax.shard_map(
        shards,
        mesh=mesh,
        in_specs=placed,
        out_specs=(P(None, "cls", "cell"), P(("cell", "cls"), None)),
        check_vma=False,
    )
```

```python
import functools

import jax
import jax.numpy as jnp
from jax import lax
from jax.experimental import pallas as pl
from jax.experimental.pallas import tpu as pltpu
from jax.sharding import PartitionSpec as P

MESH = pl.DeviceIdType.MESH
F32 = jnp.float32
BF16 = jnp.bfloat16
NODES = 64
CLASSES = 32
SIDE = 16
PLANE = 256
LAYERS = 4
BLOCK = LAYERS * PLANE
KC = 8
NCELLS = 65536
COUNT_SCALE = 400.0
CHUNKS = 8
GROUPS = 8
FIRST = 4


HALO = ((0, 1), (1, 1), (2, 1), (3, 1), (5, 1), (0, 2), (1, 2), (3, 2), (1, 3))
REST = ((4, 1), (2, 2), (0, 3))
HALO_ROWS = len(HALO) + 1
REST_ROWS = len(REST)
OWN_ROWS = 8 * LAYERS + 1


def split2(x):
    hi = x.astype(BF16)
    return hi, (x - hi.astype(F32)).astype(BF16)


def dot_nn(a, b):
    return jnp.dot(a, b, preferred_element_type=F32)


def dot3(a, b):
    (ah, al), (bh, bl) = a, b
    return dot_nn(ah, bh) + (dot_nn(al, bh) + dot_nn(ah, bl))


def main_kernel(
    melt_hbm, counts_hbm, pres_ref, prop_hbm, coup_hbm, fw_hbm,
    m_ref, walls_ref, vec_ref, pout_ref,
    melt_v, counts_ref, prop_v, coup_v, fw_v, own, halo, halo_out, rest, rest_out, acc, srow, pbuf,
    load_sem, small_sem, own_send, own_recv, halo_send, halo_recv, rest_send, rest_recv, s_send, s_recv, ready,
):
    cell = lax.axis_index("cell")
    cls = lax.axis_index("cls")
    core = lax.rem(cell, 2)
    yy = lax.rem(lax.div(cell, 2), 4)
    zh = lax.rem(lax.div(cell, 8), 2)
    xx = lax.div(cell, 16)
    has_prev = cell > 0
    has_next = cell < 63

    loads = [
        pltpu.make_async_copy(melt_hbm.at[:, pl.ds(i * 128, 128)], melt_v.at[i], load_sem.at[i])
        for i in range(CHUNKS)
    ]
    smalls = [
        pltpu.make_async_copy(prop_hbm.at[pl.ds(cls * 512, 512)], prop_v, small_sem.at[0]),
        pltpu.make_async_copy(coup_hbm.at[pl.ds(cls * 8, 8)], coup_v, small_sem.at[1]),
        pltpu.make_async_copy(fw_hbm.at[pl.ds(cls * 8, 8)], fw_v, small_sem.at[2]),
        pltpu.make_async_copy(counts_hbm, counts_ref, small_sem.at[3]),
        pltpu.make_async_copy(pres_ref, own.at[cls, OWN_ROWS - 1], small_sem.at[4]),
        pltpu.make_async_copy(pres_ref, halo_out.at[0, HALO_ROWS - 1], small_sem.at[5]),
        pltpu.make_async_copy(pres_ref, halo_out.at[1, HALO_ROWS - 1], small_sem.at[6]),
    ]
    for copy in smalls + loads:
        copy.start()

    barrier = pltpu.get_barrier_semaphore()

    def signal(c, k):
        pl.semaphore_signal(barrier, inc=1, device_id=(c, k), device_id_type=MESH)

    def block_at(x, z, y, c):
        return ((x * 2 + z) * 4 + y) * 2 + c

    adds = jnp.logical_or(cls == 0, cls == 3)
    second = jnp.where(cls == 0, 1, 2)
    near = jnp.where(cls < 2, 3, 0)
    near2 = jnp.where(cls == 3, 1, 2)
    server = jnp.where(cls < 2, 0, 3)
    one = jnp.int32(1)

    @pl.when(has_prev)
    def _():
        for k in range(4):
            signal(cell - 1, k)

    @pl.when(has_next)
    def _():
        for k in range(4):
            signal(cell + 1, k)

    for d in range(4):
        signal(block_at(lax.rem(xx + d, 4), 1 - zh, yy, core), near)
    for d in range(1, 4):
        signal(cell, lax.rem(cls + d, 4))
    for d in range(1, 4):
        signal(block_at(lax.rem(xx + d, 4), zh, yy, core), server)
    for d in range(1, 8):
        signal(lax.div(cell, 8) * 8 + lax.rem(cell + d, 8), cls)

    @pl.when(adds)
    def _():
        for d in range(4):
            signal(block_at(lax.rem(xx + d, 4), 1 - zh, yy, core), near2)
        for d in range(1, 4):
            signal(block_at(lax.rem(xx + d, 4), zh, yy, core), second)

    greeted = 17 + 7 * jnp.where(adds, one, 0) + 4 * jnp.where(has_prev, one, 0) + 4 * jnp.where(has_next, one, 0)

    def own_copy(k):
        return pltpu.make_async_remote_copy(
            src_ref=own.at[cls], dst_ref=own.at[cls], send_sem=own_send.at[k], recv_sem=own_recv.at[cls],
            device_id=(cell, k), device_id_type=MESH)

    def halo_copy(side, k):
        return pltpu.make_async_remote_copy(
            src_ref=halo_out.at[side], dst_ref=halo.at[1 - side, cls], send_sem=halo_send.at[side, k],
            recv_sem=halo_recv.at[1 - side, cls], device_id=(cell + (2 * side - 1), k), device_id_type=MESH)

    def rest_copy(side):
        return pltpu.make_async_remote_copy(
            src_ref=rest_out.at[side], dst_ref=rest.at[1 - side, cls], send_sem=rest_send.at[side],
            recv_sem=rest_recv.at[1 - side, cls], device_id=(cell + (2 * side - 1), 3 - 3 * side), device_id_type=MESH)

    def each_rest(act):
        @pl.when(has_prev)
        def _():
            act(rest_copy(0))

        @pl.when(has_next)
        def _():
            act(rest_copy(1))

    takes_rest = (jnp.logical_and(has_prev, cls == 0), jnp.logical_and(has_next, cls == 3))

    def each_copy(order, act):
        for classes in order:
            @pl.when(has_prev)
            def _(classes=classes):
                for k in classes:
                    act(halo_copy(0, k))

            @pl.when(has_next)
            def _(classes=classes):
                for k in classes:
                    act(halo_copy(1, k))

            for k in classes:
                @pl.when(cls != k)
                def _(k=k):
                    act(own_copy(k))

    for side in range(2):
        @pl.when(jnp.logical_not(takes_rest[side]))
        def _(side=side):
            rest[side] = jnp.zeros((4, REST_ROWS, 1, PLANE), F32)

    halo[2] = jnp.zeros((4, HALO_ROWS, 1, PLANE), F32)
    in_group = lax.rem(cell, 8)
    waits_across = zh == 1
    there = (has_prev, has_next)
    crosses = (jnp.logical_and(has_prev, in_group == 0), jnp.logical_and(has_next, in_group == 7))
    later = tuple(jnp.logical_and(c, waits_across) for c in crosses)
    soon = tuple(jnp.logical_and(t, jnp.logical_not(l)) for t, l in zip(there, later))
    adds_across = jnp.logical_and(jnp.logical_or(crosses[0], crosses[1]), jnp.logical_not(waits_across))
    across_slot = jnp.where(adds_across, jnp.where(crosses[1], 1, 0), 2)

    for copy in smalls:
        copy.wait()
    prop = prop_v[...]
    p_hi, p_lo = split2(prop)
    pp = jnp.concatenate([p_hi, p_lo], axis=1)
    lane = lax.broadcasted_iota(jnp.int32, (KC, 128), 1)
    row = lax.broadcasted_iota(jnp.int32, (KC, 128), 0)
    half = jnp.where(lane >= 64, 1, 0)

    def doubled(x):
        return jnp.concatenate([x, x], axis=1)

    def kron(x):
        return jnp.concatenate([jnp.where(row == 2 * v + half, x, 0.0) for v in range(4)], axis=1)

    def spread(r):
        return jnp.concatenate(split2(kron(r)), axis=0)

    def row_step(wide):
        y = dot_nn(wide, pp)
        y = y[:KC] + y[KC:]
        return y + pltpu.roll(y, 64, 1)

    fw = fw_v[...]
    coup = coup_v[...]
    wide_lane = lax.broadcasted_iota(jnp.int32, (NODES, NODES * KC), 1)
    wide_row = lax.broadcasted_iota(jnp.int32, (NODES, NODES * KC), 0)
    repeat8 = jnp.where(wide_lane // KC == wide_row, 1.0, 0.0).astype(BF16)
    own_class = (wide_lane % KC == wide_row % KC)[: 2 * KC]

    def flux_rows(r):
        both = jnp.concatenate(split2(r[:, :NODES]), axis=0)
        return jnp.where(own_class, dot_nn(both, repeat8), 0.0).astype(BF16)

    rs = [doubled(fw)]
    flux_w = []
    for t in range(4):
        rs.append(row_step(spread(rs[-1])))
        flux_w.append(flux_rows(rs[-1]))
    weights_f = jnp.concatenate(flux_w, axis=0)

    counts_f = counts_ref[...].astype(F32)
    flux = [[] for _ in range(4)]
    for n in range(CHUNKS // 2):
        loads[2 * n].wait()
        loads[2 * n + 1].wait()
        pair = jnp.concatenate([melt_v[2 * n], melt_v[2 * n + 1]], axis=1)
        y = dot_nn(weights_f, pair.astype(BF16))
        for t in range(4):
            flux[t].append(y[16 * t : 16 * t + 8] + y[16 * t + 8 : 16 * t + 16])
    scale = 1.0 / (COUNT_SCALE * CLASSES)

    def put(r, value):
        for l in range(LAYERS):
            tile = value[:, l * PLANE : (l + 1) * PLANE]
            own[cls, r * LAYERS + l] = tile
            if (r, l + 1) in HALO:
                halo_out[0, HALO.index((r, l + 1))] = tile
            if (r, LAYERS - l) in HALO:
                halo_out[1, HALO.index((r, LAYERS - l))] = tile
            if (r, l + 1) in REST:
                rest_out[0, REST.index((r, l + 1))] = tile
            if (r, LAYERS - l) in REST:
                rest_out[1, REST.index((r, LAYERS - l))] = tile

    for t in range(4):
        a_t = jnp.sum(rs[t][:, :NODES] * coup, axis=1, keepdims=True)
        put(2 * t + 1, jnp.sum(counts_f * a_t, axis=0, keepdims=True) * scale)
    for t in range(4):
        put(2 * t, jnp.sum(counts_f * jnp.concatenate(flux[t], axis=1), axis=0, keepdims=True) * scale)

    pl.semaphore_wait(barrier, greeted)
    each_copy(((0, 3),), lambda copy: copy.start())

    def announce(c, k):
        pl.semaphore_signal(ready, inc=1, device_id=(c, k), device_id_type=MESH)

    for d in range(1, 4):
        announce(block_at(lax.rem(xx + d, 4), zh, yy, core), server)
    for d in range(4):
        announce(block_at(lax.rem(xx + d, 4), 1 - zh, yy, core), near)

    @pl.when(jnp.logical_not(adds))
    def _():
        announce(cell, server)

    def col_step(v):
        hi, lo = split2(v[:, :NODES])
        lhs = jnp.concatenate([hi, lo], axis=0)
        nt = (((1,), (1,)), ((), ()))
        y = lax.dot_general(lhs, p_hi, nt, preferred_element_type=F32)
        y = y[:KC] + y[KC:] + lax.dot_general(hi, p_lo, nt, preferred_element_type=F32)
        z = jnp.zeros((KC, 128), F32)
        for q in range(4):
            z = z + jnp.where(row == 2 * q + half, y[:, 128 * q : 128 * (q + 1)], 0.0)
        return z + pltpu.roll(z, 64, 1)

    vs = [doubled(coup)]
    for s in range(3):
        vs.append(col_step(vs[-1]))
    for s in range(4):
        for j in range(NODES):
            vec_ref[s, pl.ds(j * KC, KC), :] = jnp.broadcast_to(vs[3 - s][:, j : j + 1], (KC, 128))

    def powers_into_melt(classes):
        for k in classes:
            base = split2(prop_v[pl.ds(k * NODES, NODES), :])
            two = split2(dot3(base, base))
            four_hi, four_lo = split2(dot3(two, two))
            lhs = jnp.concatenate([four_hi, four_hi, four_lo], axis=1)
            at = pl.ds(k, NODES, stride=KC)
            for n in range(CHUNKS // 2):
                x = jnp.concatenate([melt_v[2 * n, at, :], melt_v[2 * n + 1, at, :]], axis=1)
                x_hi, x_lo = split2(x)
                y = dot_nn(lhs, jnp.concatenate([x_hi, x_lo, x_hi], axis=0))
                m_ref[2 * n, at, :] = y[:, :128]
                m_ref[2 * n + 1, at, :] = y[:, 128:]

    powers_into_melt(range(0, 3))
    each_copy(((1, 2),), lambda copy: copy.start())
    each_rest(lambda copy: copy.start())
    powers_into_melt(range(3, FIRST))

    for d in range(1, 4):
        k = lax.rem(cls + d, 4)
        pltpu.make_async_copy(own.at[k], own.at[k], own_recv.at[k]).wait()
    def wait_halo(sides):
        for side in range(2):
            @pl.when(sides[side])
            def _(side=side):
                for k in range(4):
                    pltpu.make_async_copy(halo.at[side, k], halo.at[side, k], halo_recv.at[side, k]).wait()

    wait_halo(soon)

    lane2 = lax.broadcasted_iota(jnp.int32, (KC, PLANE), 1)
    row2 = lax.broadcasted_iota(jnp.int32, (KC, PLANE), 0)

    def plane_neighbours(x):
        west = jnp.where(lane2 % SIDE == 0, 0.0, pltpu.roll(x, 1, 1))
        east = jnp.where(lane2 % SIDE == SIDE - 1, 0.0, pltpu.roll(x, PLANE - 1, 1))
        north = jnp.where(lane2 < SIDE, 0.0, pltpu.roll(x, SIDE, 1))
        south = jnp.where(lane2 >= PLANE - SIDE, 0.0, pltpu.roll(x, PLANE - SIDE, 1))
        return west + east + (north + south)

    def halo_field(slot, r, d):
        rows = [halo[slot, k, HALO.index((r, d))] for k in range(4)]
        return jnp.broadcast_to(rows[0] + rows[1] + (rows[2] + rows[3]), (KC, PLANE))

    class Recurrence:
        def __init__(self, sides):
            self.slots = [jnp.where(sides[side], side, 2) for side in range(2)]
            self.inside = [jnp.where(sides[side], 1.0, 0.0).astype(F32) for side in range(2)]
            self.fields = {}
            self.gases = [{} for _ in range(4)]
            self.states = [{} for _ in range(5)]
            for layer in range(-4, 8):
                p = jnp.broadcast_to(self.start_pressure(layer), (KC, PLANE))
                self.states[0][layer] = jnp.where(row2 == 0, p, 0.0)

        def start_pressure(self, layer):
            if 0 <= layer < LAYERS:
                return own[layer, OWN_ROWS - 1]
            side, k = (0, layer + 4) if layer < 0 else (1, layer - LAYERS)
            return halo[self.slots[side], k, HALO_ROWS - 1]

        def field(self, layer, r):
            if (layer, r) not in self.fields:
                if 0 <= layer < LAYERS:
                    rows = [own[k, r * LAYERS + layer] for k in range(4)]
                    value = jnp.broadcast_to(rows[0] + rows[1] + (rows[2] + rows[3]), (KC, PLANE))
                else:
                    side, d = (0, -layer) if layer < 0 else (1, layer - LAYERS + 1)
                    if (r, d) in HALO:
                        value = halo_field(self.slots[side], r, d)
                    else:
                        rows = [rest[side, k, REST.index((r, d))] for k in range(4)]
                        value = jnp.broadcast_to(rows[0] + rows[1] + (rows[2] + rows[3]), (KC, PLANE))
                self.fields[layer, r] = value
            return self.fields[layer, r]

        def add_gas(self, s, layers):
            for layer in layers:
                g = jnp.where(row2 == 0, self.field(layer, 2 * s), 0.0)
                for m in range(s + 1):
                    g = g + self.field(layer, 2 * m + 1) * (0.5 * self.states[s - m][layer])
                self.gases[s][layer] = g

        def advance(self, s, layers):
            now = self.states[s]
            for layer in layers:
                x = now[layer]
                around = plane_neighbours(x) + (now[layer - 1] + now[layer + 1])
                x = x + 0.15 * (around - 6.0 * x) + 0.1 * self.gases[s][layer] - 0.2 * x
                x = x + jnp.where(row2 == s + 1, 0.2, 0.0)
                if layer < 0:
                    x = x * self.inside[0]
                if layer >= LAYERS:
                    x = x * self.inside[1]
                self.states[s + 1][layer] = x

        def main_part(self):
            for s in range(3):
                reach = range(s - 2, LAYERS + 2 - s)
                self.add_gas(s, reach)
                self.advance(s, reach)
            self.add_gas(3, range(LAYERS))

        def last_pressure(self):
            for s in range(3):
                ends = (s - 3, LAYERS + 2 - s)
                self.add_gas(s, ends)
                self.advance(s, ends)
            self.advance(3, range(LAYERS))

    quick = Recurrence(soon)
    quick.main_part()
    gases = quick.gases

    extra = [{} for _ in range(4)]
    shift = [{} for _ in range(4)]
    for s in range(1, 4):
        for d in range(1, s + 1):
            if d == 1:
                inner = jnp.where(crosses[1], quick.states[s - 1][LAYERS - 1], quick.states[s - 1][0])
            else:
                inner = shift[s - 1][d - 1]
            y = 0.15 * inner
            if d in shift[s - 1]:
                x = shift[s - 1][d]
                around = plane_neighbours(x)
                if d + 1 in shift[s - 1]:
                    around = around + shift[s - 1][d + 1]
                y = y + (x + 0.15 * (around - 6.0 * x) + 0.1 * extra[s - 1][d] - 0.2 * x)
            shift[s][d] = y
            g = jnp.zeros((KC, PLANE), F32)
            for m in range(s):
                if d in shift[s - m]:
                    g = g + halo_field(across_slot, 2 * m + 1, d) * (0.5 * shift[s - m][d])
            extra[s][d] = g

    packed = jnp.zeros((KC, 128), F32)
    for s in range(4):
        t = gases[s][0] + gases[s][1] + (gases[s][2] + gases[s][3])
        for d in extra[s]:
            t = t + extra[s][d]
        t = jnp.sum(t[:, :128] + t[:, 128:], axis=1, keepdims=True)
        packed = packed + jnp.where(jnp.logical_and(lane == s * 4 + row, row < 4), t, 0.0)
    packed = jnp.sum(packed, axis=0, keepdims=True)
    slot = (xx * 4 + yy) * 2 + core
    srow[0] = packed
    acc[zh * 32 + slot] = packed

    hops = [0, 1, 2, 1]
    offsets = sorted(
        ((dx, dy, dc) for dx in range(4) for dy in range(4) for dc in range(2)),
        key=lambda o: -(hops[o[0]] + hops[o[1]] + 0.3 * o[2]),
    )

    def block_of(o, z):
        return block_at(lax.rem(xx + o[0], 4), z, lax.rem(yy + o[1], 4), lax.rem(core + o[2], 2))

    def sum_copy(c, k, sem, arrived):
        return pltpu.make_async_remote_copy(
            src_ref=srow.at[0], dst_ref=acc.at[zh * 32 + slot], send_sem=sem, recv_sem=arrived,
            device_id=(c, k), device_id_type=MESH)

    @pl.when(adds)
    def _():
        pl.semaphore_wait(ready, 15)
        for o in offsets:
            sum_copy(block_of(o, 1 - zh), near2, s_send.at[2], s_recv.at[1]).start()
            sum_copy(block_of(o, 1 - zh), near, s_send.at[1], s_recv.at[1]).start()
            if o != (0, 0, 0):
                sum_copy(block_of(o, zh), second, s_send.at[3], s_recv.at[0]).start()
                sum_copy(block_of(o, zh), cls, s_send.at[0], s_recv.at[0]).start()

    powers_into_melt(range(FIRST, KC))
    for side in range(2):
        @pl.when(takes_rest[side])
        def _(side=side):
            for k in range(4):
                pltpu.make_async_copy(rest.at[side, k], rest.at[side, k], rest_recv.at[side, k]).wait()

    wait_halo(later)
    exact = Recurrence(there)
    exact.main_part()
    exact.last_pressure()
    states = exact.states
    first31 = acc.at[pl.ds(0, 31)]
    first32 = acc.at[pl.ds(0, 32)]
    pltpu.make_async_copy(first31, first31, s_recv.at[0]).wait()
    pltpu.make_async_copy(first32, first32, s_recv.at[1]).wait()
    total = jnp.sum(acc[...], axis=0)

    def coefficient(s, r):
        return total[:, s * 4 + r : s * 4 + r + 1]

    chambers = []
    for s in range(4):
        t = coefficient(s, 0)
        for r in range(s):
            t = t + chambers[r] * coefficient(s, r + 1)
        chambers.append(1.5 - 0.5 * (t / NCELLS))
    weights = jnp.where(row2 == 0, 1.0, 0.0)
    for r in range(3):
        weights = jnp.where(row2 == r + 1, chambers[r], weights)

    for layer in range(LAYERS):
        at = pl.ds(layer * PLANE, PLANE)
        for s in range(4):
            walls_ref[s : s + 1, at] = 0.5 * jnp.sum(weights * states[s][layer], axis=0, keepdims=True)
        pbuf[layer] = jnp.sum(weights * states[4][layer], axis=0, keepdims=True) + 0.2 * chambers[3]
    pout_ref[...] = pbuf[cls]

    each_copy(((0, 3), (1, 2)), lambda copy: copy.wait_send())
    each_rest(lambda copy: copy.wait_send())

    @pl.when(adds)
    def _():
        pltpu.make_async_copy(first31, first31, s_send.at[0]).wait()
        pltpu.make_async_copy(first32, first32, s_send.at[1]).wait()
        pltpu.make_async_copy(first32, first32, s_send.at[2]).wait()
        pltpu.make_async_copy(first31, first31, s_send.at[3]).wait()


def finish_kernel(m_ref, walls_ref, vec_ref, p_ref, out_hbm, pout_hbm, out_v, sem):
    p_out = pltpu.make_async_copy(p_ref, pout_hbm, sem.at[GROUPS])
    p_out.start()
    walls = [
        [jnp.broadcast_to(walls_ref[s : s + 1, i * 128 : (i + 1) * 128], (KC, 128)) for i in range(CHUNKS)]
        for s in range(4)
    ]
    copies = [p_out]
    step = NODES // GROUPS
    for g in range(GROUPS):
        for j in range(g * step, (g + 1) * step):
            at = pl.ds(j * KC, KC)
            v = [vec_ref[s, at, :] for s in range(4)]
            for i in range(CHUNKS):
                y = m_ref[i, at, :]
                for s in range(4):
                    y = y + v[s] * walls[s][i]
                out_v[at, pl.ds(i * 128, 128)] = y
        rows = pl.ds(g * step * KC, step * KC)
        copies.append(pltpu.make_async_copy(out_v.at[rows], out_hbm.at[rows], sem.at[g]))
        copies[-1].start()
    for copy in copies:
        copy.wait()


def shards(melt, counts, pressure, propagator, coupling, flux_weights):
    vmem = pl.BlockSpec(memory_space=pltpu.VMEM)
    hbm = pl.BlockSpec(memory_space=pltpu.HBM)
    dma = pltpu.SemaphoreType.DMA
    m, walls, vec, pout = pl.pallas_call(
        main_kernel,
        name="block_step",
        out_shape=(
            jax.ShapeDtypeStruct((CHUNKS, NODES * KC, 128), F32),
            jax.ShapeDtypeStruct((4, BLOCK), F32),
            jax.ShapeDtypeStruct((4, NODES * KC, 128), F32),
            jax.ShapeDtypeStruct((1, PLANE), F32),
        ),
        in_specs=[hbm] * 6,
        out_specs=(vmem, vmem, vmem, vmem),
        scratch_shapes=[
            pltpu.VMEM((CHUNKS, NODES * KC, 128), F32),
            pltpu.VMEM((KC, BLOCK), jnp.int32),
            pltpu.VMEM((KC * NODES, NODES), F32),
            pltpu.VMEM((KC, NODES), F32),
            pltpu.VMEM((KC, NODES), F32),
            pltpu.VMEM((4, OWN_ROWS, 1, PLANE), F32),
            pltpu.VMEM((3, 4, HALO_ROWS, 1, PLANE), F32),
            pltpu.VMEM((2, HALO_ROWS, 1, PLANE), F32),
            pltpu.VMEM((2, 4, REST_ROWS, 1, PLANE), F32),
            pltpu.VMEM((2, REST_ROWS, 1, PLANE), F32),
            pltpu.VMEM((64, 1, 128), F32),
            pltpu.VMEM((1, 1, 128), F32),
            pltpu.VMEM((LAYERS, 1, PLANE), F32),
            dma((CHUNKS,)), dma((7,)),
            dma((4,)), dma((4,)), dma((2, 4)), dma((2, 4)), dma((2,)), dma((2, 4)),
            dma((4,)), dma((2,)), pltpu.SemaphoreType.REGULAR,
        ],
        compiler_params=pltpu.CompilerParams(collective_id=0, has_side_effects=True, vmem_limit_bytes=32 << 20),
    )(
        *(
            pltpu.with_memory_space_constraint(x, pltpu.HBM)
            for x in (
                melt.reshape(NODES * KC, BLOCK), counts, pressure,
                propagator.reshape(CLASSES * NODES, NODES), coupling, flux_weights,
            )
        )
    )
    shells, pout = pl.pallas_call(
        finish_kernel,
        name="walls_into_shells",
        out_shape=(
            jax.ShapeDtypeStruct((NODES * KC, BLOCK), F32),
            jax.ShapeDtypeStruct((1, PLANE), F32),
        ),
        in_specs=[vmem, vmem, vmem, vmem],
        out_specs=(hbm, hbm),
        scratch_shapes=[pltpu.VMEM((NODES * KC, BLOCK), F32), dma((GROUPS + 1,))],
        compiler_params=pltpu.CompilerParams(vmem_limit_bytes=32 << 20),
    )(m, walls, vec, pout)
    return shells.reshape(NODES, KC, BLOCK), pout


def solution(mesh):
    placed = (P(None, "cls", "cell"), P("cls", "cell"), P(("cell", "cls"), None), P(), P(), P())
    return jax.shard_map(
        shards,
        mesh=mesh,
        in_specs=placed,
        out_specs=(P(None, "cls", "cell"), P(("cell", "cls"), None)),
        check_vma=False,
    )
```

```python
import functools

import jax
import jax.numpy as jnp
from jax import lax
from jax.experimental import pallas as pl
from jax.experimental.pallas import tpu as pltpu
from jax.sharding import PartitionSpec as P

MESH = pl.DeviceIdType.MESH
F32 = jnp.float32
BF16 = jnp.bfloat16
NODES = 64
CLASSES = 32
SIDE = 16
PLANE = 256
LAYERS = 4
BLOCK = LAYERS * PLANE
KC = 8
NCELLS = 65536
COUNT_SCALE = 400.0
CHUNKS = 8
GROUPS = 8
FIRST = 4


HALO = ((0, 1), (1, 1), (2, 1), (3, 1), (5, 1), (0, 2), (1, 2), (3, 2), (1, 3))
REST = ((4, 1), (2, 2), (0, 3))
HALO_ROWS = len(HALO) + 1
REST_ROWS = len(REST)
OWN_ROWS = 8 * LAYERS + 1


def split2(x):
    hi = x.astype(BF16)
    return hi, (x - hi.astype(F32)).astype(BF16)


def dot_nn(a, b):
    return jnp.dot(a, b, preferred_element_type=F32)


def dot3(a, b):
    (ah, al), (bh, bl) = a, b
    return dot_nn(ah, bh) + (dot_nn(al, bh) + dot_nn(ah, bl))


def main_kernel(
    melt_hbm, counts_hbm, pres_ref, prop_hbm, coup_hbm, fw_hbm,
    m_ref, walls_ref, vec_ref, pout_ref,
    melt_v, counts_ref, prop_v, coup_v, fw_v, own, halo, halo_out, rest, rest_out, acc, srow, pbuf,
    load_sem, small_sem, own_send, own_recv, halo_send, halo_recv, rest_send, rest_recv, s_send, s_recv, ready,
):
    cell = lax.axis_index("cell")
    cls = lax.axis_index("cls")
    core = lax.rem(cell, 2)
    yy = lax.rem(lax.div(cell, 2), 4)
    zh = lax.rem(lax.div(cell, 8), 2)
    xx = lax.div(cell, 16)
    has_prev = cell > 0
    has_next = cell < 63

    loads = [
        pltpu.make_async_copy(melt_hbm.at[:, pl.ds(i * 128, 128)], melt_v.at[i], load_sem.at[i])
        for i in range(CHUNKS)
    ]
    smalls = [
        pltpu.make_async_copy(prop_hbm.at[pl.ds(cls * 512, 512)], prop_v, small_sem.at[0]),
        pltpu.make_async_copy(coup_hbm.at[pl.ds(cls * 8, 8)], coup_v, small_sem.at[1]),
        pltpu.make_async_copy(fw_hbm.at[pl.ds(cls * 8, 8)], fw_v, small_sem.at[2]),
        pltpu.make_async_copy(counts_hbm, counts_ref, small_sem.at[3]),
        pltpu.make_async_copy(pres_ref, own.at[cls, OWN_ROWS - 1], small_sem.at[4]),
        pltpu.make_async_copy(pres_ref, halo_out.at[0, HALO_ROWS - 1], small_sem.at[5]),
        pltpu.make_async_copy(pres_ref, halo_out.at[1, HALO_ROWS - 1], small_sem.at[6]),
    ]
    for copy in smalls + loads:
        copy.start()

    barrier = pltpu.get_barrier_semaphore()

    def signal(c, k):
        pl.semaphore_signal(barrier, inc=1, device_id=(c, k), device_id_type=MESH)

    def block_at(x, z, y, c):
        return ((x * 2 + z) * 4 + y) * 2 + c

    adds = jnp.logical_or(cls == 0, cls == 3)
    second = jnp.where(cls == 0, 1, 2)
    near = jnp.where(cls < 2, 3, 0)
    near2 = jnp.where(cls == 3, 1, 2)
    server = jnp.where(cls < 2, 0, 3)
    one = jnp.int32(1)

    @pl.when(has_prev)
    def _():
        for k in range(4):
            signal(cell - 1, k)

    @pl.when(has_next)
    def _():
        for k in range(4):
            signal(cell + 1, k)

    for d in range(4):
        signal(block_at(lax.rem(xx + d, 4), 1 - zh, yy, core), near)
    for d in range(1, 4):
        signal(cell, lax.rem(cls + d, 4))
    for d in range(1, 4):
        signal(block_at(lax.rem(xx + d, 4), zh, yy, core), server)
    for d in range(1, 8):
        signal(lax.div(cell, 8) * 8 + lax.rem(cell + d, 8), cls)

    @pl.when(adds)
    def _():
        for d in range(4):
            signal(block_at(lax.rem(xx + d, 4), 1 - zh, yy, core), near2)
        for d in range(1, 4):
            signal(block_at(lax.rem(xx + d, 4), zh, yy, core), second)

    greeted = 17 + 7 * jnp.where(adds, one, 0) + 4 * jnp.where(has_prev, one, 0) + 4 * jnp.where(has_next, one, 0)

    def own_copy(k):
        return pltpu.make_async_remote_copy(
            src_ref=own.at[cls], dst_ref=own.at[cls], send_sem=own_send.at[k], recv_sem=own_recv.at[cls],
            device_id=(cell, k), device_id_type=MESH)

    def halo_copy(side, k):
        return pltpu.make_async_remote_copy(
            src_ref=halo_out.at[side], dst_ref=halo.at[1 - side, cls], send_sem=halo_send.at[side, k],
            recv_sem=halo_recv.at[1 - side, cls], device_id=(cell + (2 * side - 1), k), device_id_type=MESH)

    def rest_copy(side):
        return pltpu.make_async_remote_copy(
            src_ref=rest_out.at[side], dst_ref=rest.at[1 - side, cls], send_sem=rest_send.at[side],
            recv_sem=rest_recv.at[1 - side, cls], device_id=(cell + (2 * side - 1), 3 - 3 * side), device_id_type=MESH)

    def each_rest(act):
        @pl.when(has_prev)
        def _():
            act(rest_copy(0))

        @pl.when(has_next)
        def _():
            act(rest_copy(1))

    takes_rest = (jnp.logical_and(has_prev, cls == 0), jnp.logical_and(has_next, cls == 3))

    def each_copy(order, act):
        for classes in order:
            @pl.when(has_prev)
            def _(classes=classes):
                for k in classes:
                    act(halo_copy(0, k))

            @pl.when(has_next)
            def _(classes=classes):
                for k in classes:
                    act(halo_copy(1, k))

            for k in classes:
                @pl.when(cls != k)
                def _(k=k):
                    act(own_copy(k))

    for side in range(2):
        @pl.when(jnp.logical_not(takes_rest[side]))
        def _(side=side):
            rest[side] = jnp.zeros((4, REST_ROWS, 1, PLANE), F32)

    halo[2] = jnp.zeros((4, HALO_ROWS, 1, PLANE), F32)
    in_group = lax.rem(cell, 8)
    waits_across = zh == 1
    there = (has_prev, has_next)
    crosses = (jnp.logical_and(has_prev, in_group == 0), jnp.logical_and(has_next, in_group == 7))
    later = tuple(jnp.logical_and(c, waits_across) for c in crosses)
    soon = tuple(jnp.logical_and(t, jnp.logical_not(l)) for t, l in zip(there, later))
    adds_across = jnp.logical_and(jnp.logical_or(crosses[0], crosses[1]), jnp.logical_not(waits_across))
    across_slot = jnp.where(adds_across, jnp.where(crosses[1], 1, 0), 2)

    for copy in smalls:
        copy.wait()
    prop = prop_v[...]
    p_hi, p_lo = split2(prop)
    pp = jnp.concatenate([p_hi, p_lo], axis=1)
    lane = lax.broadcasted_iota(jnp.int32, (KC, 128), 1)
    row = lax.broadcasted_iota(jnp.int32, (KC, 128), 0)
    half = jnp.where(lane >= 64, 1, 0)

    def doubled(x):
        return jnp.concatenate([x, x], axis=1)

    def kron(x):
        return jnp.concatenate([jnp.where(row == 2 * v + half, x, 0.0) for v in range(4)], axis=1)

    def spread(r):
        return jnp.concatenate(split2(kron(r)), axis=0)

    def row_step(wide):
        y = dot_nn(wide, pp)
        y = y[:KC] + y[KC:]
        return y + pltpu.roll(y, 64, 1)

    fw = fw_v[...]
    coup = coup_v[...]
    wide_lane = lax.broadcasted_iota(jnp.int32, (NODES, NODES * KC), 1)
    wide_row = lax.broadcasted_iota(jnp.int32, (NODES, NODES * KC), 0)
    repeat8 = jnp.where(wide_lane // KC == wide_row, 1.0, 0.0).astype(BF16)
    own_class = (wide_lane % KC == wide_row % KC)[: 2 * KC]

    def flux_rows(r):
        both = jnp.concatenate(split2(r[:, :NODES]), axis=0)
        return jnp.where(own_class, dot_nn(both, repeat8), 0.0).astype(BF16)

    rs = [doubled(fw)]
    flux_w = []
    for t in range(4):
        rs.append(row_step(spread(rs[-1])))
        flux_w.append(flux_rows(rs[-1]))
    weights_f = jnp.concatenate(flux_w, axis=0)

    counts_f = counts_ref[...].astype(F32)
    flux = [[] for _ in range(4)]
    for n in range(CHUNKS // 2):
        loads[2 * n].wait()
        loads[2 * n + 1].wait()
        pair = jnp.concatenate([melt_v[2 * n], melt_v[2 * n + 1]], axis=1)
        y = dot_nn(weights_f, pair.astype(BF16))
        for t in range(4):
            flux[t].append(y[16 * t : 16 * t + 8] + y[16 * t + 8 : 16 * t + 16])
    scale = 1.0 / (COUNT_SCALE * CLASSES)

    def put(r, value):
        for l in range(LAYERS):
            tile = value[:, l * PLANE : (l + 1) * PLANE]
            own[cls, r * LAYERS + l] = tile
            if (r, l + 1) in HALO:
                halo_out[0, HALO.index((r, l + 1))] = tile
            if (r, LAYERS - l) in HALO:
                halo_out[1, HALO.index((r, LAYERS - l))] = tile
            if (r, l + 1) in REST:
                rest_out[0, REST.index((r, l + 1))] = tile
            if (r, LAYERS - l) in REST:
                rest_out[1, REST.index((r, LAYERS - l))] = tile

    for t in range(4):
        a_t = jnp.sum(rs[t][:, :NODES] * coup, axis=1, keepdims=True)
        put(2 * t + 1, jnp.sum(counts_f * a_t, axis=0, keepdims=True) * scale)
    for t in range(4):
        put(2 * t, jnp.sum(counts_f * jnp.concatenate(flux[t], axis=1), axis=0, keepdims=True) * scale)

    pl.semaphore_wait(barrier, greeted)
    each_copy(((0, 3),), lambda copy: copy.start())

    def announce(c, k):
        pl.semaphore_signal(ready, inc=1, device_id=(c, k), device_id_type=MESH)

    for d in range(1, 4):
        announce(block_at(lax.rem(xx + d, 4), zh, yy, core), server)
    for d in range(4):
        announce(block_at(lax.rem(xx + d, 4), 1 - zh, yy, core), near)

    @pl.when(jnp.logical_not(adds))
    def _():
        announce(cell, server)

    def col_step(v):
        hi, lo = split2(v[:, :NODES])
        lhs = jnp.concatenate([hi, lo], axis=0)
        nt = (((1,), (1,)), ((), ()))
        y = lax.dot_general(lhs, p_hi, nt, preferred_element_type=F32)
        y = y[:KC] + y[KC:] + lax.dot_general(hi, p_lo, nt, preferred_element_type=F32)
        z = jnp.zeros((KC, 128), F32)
        for q in range(4):
            z = z + jnp.where(row == 2 * q + half, y[:, 128 * q : 128 * (q + 1)], 0.0)
        return z + pltpu.roll(z, 64, 1)

    vs = [doubled(coup)]
    for s in range(3):
        vs.append(col_step(vs[-1]))
    for s in range(4):
        for j in range(NODES):
            vec_ref[s, pl.ds(j * KC, KC), :] = jnp.broadcast_to(vs[3 - s][:, j : j + 1], (KC, 128))

    def powers_into_melt(classes):
        for k in classes:
            base = split2(prop_v[pl.ds(k * NODES, NODES), :])
            two = split2(dot3(base, base))
            four_hi, four_lo = split2(dot3(two, two))
            lhs = jnp.concatenate([four_hi, four_hi, four_lo], axis=1)
            at = pl.ds(k, NODES, stride=KC)
            for n in range(CHUNKS // 2):
                x = jnp.concatenate([melt_v[2 * n, at, :], melt_v[2 * n + 1, at, :]], axis=1)
                x_hi, x_lo = split2(x)
                y = dot_nn(lhs, jnp.concatenate([x_hi, x_lo, x_hi], axis=0))
                m_ref[2 * n, at, :] = y[:, :128]
                m_ref[2 * n + 1, at, :] = y[:, 128:]

    powers_into_melt(range(0, 3))
    each_copy(((1, 2),), lambda copy: copy.start())
    each_rest(lambda copy: copy.start())
    powers_into_melt(range(3, FIRST))

    for d in range(1, 4):
        k = lax.rem(cls + d, 4)
        pltpu.make_async_copy(own.at[k], own.at[k], own_recv.at[k]).wait()
    def wait_halo(sides):
        for side in range(2):
            @pl.when(sides[side])
            def _(side=side):
                for k in range(4):
                    pltpu.make_async_copy(halo.at[side, k], halo.at[side, k], halo_recv.at[side, k]).wait()

    wait_halo(soon)

    lane2 = lax.broadcasted_iota(jnp.int32, (KC, PLANE), 1)
    row2 = lax.broadcasted_iota(jnp.int32, (KC, PLANE), 0)

    def plane_neighbours(x):
        west = jnp.where(lane2 % SIDE == 0, 0.0, pltpu.roll(x, 1, 1))
        east = jnp.where(lane2 % SIDE == SIDE - 1, 0.0, pltpu.roll(x, PLANE - 1, 1))
        north = jnp.where(lane2 < SIDE, 0.0, pltpu.roll(x, SIDE, 1))
        south = jnp.where(lane2 >= PLANE - SIDE, 0.0, pltpu.roll(x, PLANE - SIDE, 1))
        return west + east + (north + south)

    def halo_field(slot, r, d):
        rows = [halo[slot, k, HALO.index((r, d))] for k in range(4)]
        return jnp.broadcast_to(rows[0] + rows[1] + (rows[2] + rows[3]), (KC, PLANE))

    class Recurrence:
        def __init__(self, sides):
            self.slots = [jnp.where(sides[side], side, 2) for side in range(2)]
            self.inside = [jnp.where(sides[side], 1.0, 0.0).astype(F32) for side in range(2)]
            self.fields = {}
            self.gases = [{} for _ in range(4)]
            self.states = [{} for _ in range(5)]
            for layer in range(-4, 8):
                p = jnp.broadcast_to(self.start_pressure(layer), (KC, PLANE))
                self.states[0][layer] = jnp.where(row2 == 0, p, 0.0)

        def start_pressure(self, layer):
            if 0 <= layer < LAYERS:
                return own[layer, OWN_ROWS - 1]
            side, k = (0, layer + 4) if layer < 0 else (1, layer - LAYERS)
            return halo[self.slots[side], k, HALO_ROWS - 1]

        def field(self, layer, r):
            if (layer, r) not in self.fields:
                if 0 <= layer < LAYERS:
                    rows = [own[k, r * LAYERS + layer] for k in range(4)]
                    value = jnp.broadcast_to(rows[0] + rows[1] + (rows[2] + rows[3]), (KC, PLANE))
                else:
                    side, d = (0, -layer) if layer < 0 else (1, layer - LAYERS + 1)
                    if (r, d) in HALO:
                        value = halo_field(self.slots[side], r, d)
                    else:
                        rows = [rest[side, k, REST.index((r, d))] for k in range(4)]
                        value = jnp.broadcast_to(rows[0] + rows[1] + (rows[2] + rows[3]), (KC, PLANE))
                self.fields[layer, r] = value
            return self.fields[layer, r]

        def add_gas(self, s, layers):
            for layer in layers:
                g = jnp.where(row2 == 0, self.field(layer, 2 * s), 0.0)
                for m in range(s + 1):
                    g = g + self.field(layer, 2 * m + 1) * (0.5 * self.states[s - m][layer])
                self.gases[s][layer] = g

        def advance(self, s, layers):
            now = self.states[s]
            for layer in layers:
                x = now[layer]
                around = plane_neighbours(x) + (now[layer - 1] + now[layer + 1])
                x = x + 0.15 * (around - 6.0 * x) + 0.1 * self.gases[s][layer] - 0.2 * x
                x = x + jnp.where(row2 == s + 1, 0.2, 0.0)
                if layer < 0:
                    x = x * self.inside[0]
                if layer >= LAYERS:
                    x = x * self.inside[1]
                self.states[s + 1][layer] = x

        def main_part(self):
            for s in range(3):
                reach = range(s - 2, LAYERS + 2 - s)
                self.add_gas(s, reach)
                self.advance(s, reach)
            self.add_gas(3, range(LAYERS))

        def last_pressure(self):
            for s in range(3):
                ends = (s - 3, LAYERS + 2 - s)
                self.add_gas(s, ends)
                self.advance(s, ends)
            self.advance(3, range(LAYERS))

    quick = Recurrence(soon)
    quick.main_part()
    gases = quick.gases

    extra = [{} for _ in range(4)]
    shift = [{} for _ in range(4)]
    for s in range(1, 4):
        for d in range(1, s + 1):
            if d == 1:
                inner = jnp.where(crosses[1], quick.states[s - 1][LAYERS - 1], quick.states[s - 1][0])
            else:
                inner = shift[s - 1][d - 1]
            y = 0.15 * inner
            if d in shift[s - 1]:
                x = shift[s - 1][d]
                around = plane_neighbours(x)
                if d + 1 in shift[s - 1]:
                    around = around + shift[s - 1][d + 1]
                y = y + (x + 0.15 * (around - 6.0 * x) + 0.1 * extra[s - 1][d] - 0.2 * x)
            shift[s][d] = y
            g = jnp.zeros((KC, PLANE), F32)
            for m in range(s):
                if d in shift[s - m]:
                    g = g + halo_field(across_slot, 2 * m + 1, d) * (0.5 * shift[s - m][d])
            extra[s][d] = g

    packed = jnp.zeros((KC, 128), F32)
    for s in range(4):
        t = gases[s][0] + gases[s][1] + (gases[s][2] + gases[s][3])
        for d in extra[s]:
            t = t + extra[s][d]
        t = jnp.sum(t[:, :128] + t[:, 128:], axis=1, keepdims=True)
        packed = packed + jnp.where(jnp.logical_and(lane == s * 4 + row, row < 4), t, 0.0)
    packed = jnp.sum(packed, axis=0, keepdims=True)
    slot = (xx * 4 + yy) * 2 + core
    srow[0] = packed
    acc[zh * 32 + slot] = packed

    hops = [0, 1, 2, 1]
    offsets = sorted(
        ((dx, dy, dc) for dx in range(4) for dy in range(4) for dc in range(2)),
        key=lambda o: -(hops[o[0]] + hops[o[1]] + 0.3 * o[2]),
    )

    def block_of(o, z):
        return block_at(lax.rem(xx + o[0], 4), z, lax.rem(yy + o[1], 4), lax.rem(core + o[2], 2))

    def sum_copy(c, k, sem, arrived):
        return pltpu.make_async_remote_copy(
            src_ref=srow.at[0], dst_ref=acc.at[zh * 32 + slot], send_sem=sem, recv_sem=arrived,
            device_id=(c, k), device_id_type=MESH)

    @pl.when(adds)
    def _():
        pl.semaphore_wait(ready, 15)
        for o in offsets:
            sum_copy(block_of(o, 1 - zh), near2, s_send.at[2], s_recv.at[1]).start()
            sum_copy(block_of(o, 1 - zh), near, s_send.at[1], s_recv.at[1]).start()
            if o != (0, 0, 0):
                sum_copy(block_of(o, zh), second, s_send.at[3], s_recv.at[0]).start()
                sum_copy(block_of(o, zh), cls, s_send.at[0], s_recv.at[0]).start()

    powers_into_melt(range(FIRST, KC))
    for side in range(2):
        @pl.when(takes_rest[side])
        def _(side=side):
            for k in range(4):
                pltpu.make_async_copy(rest.at[side, k], rest.at[side, k], rest_recv.at[side, k]).wait()

    for i in range(CHUNKS):
        l, part_of = divmod(i * 128, PLANE)
        wall = jnp.broadcast_to(0.5 * own[l, OWN_ROWS - 1][:, part_of : part_of + 128], (KC, 128))

        def first_wall(j, carry, i=i, wall=wall):
            at = pl.ds(pl.multiple_of(j * KC, KC), KC)
            m_ref[i, at, :] = m_ref[i, at, :] + vec_ref[0, at, :] * wall
            return carry

        lax.fori_loop(0, NODES, first_wall, 0, unroll=16)

    wait_halo(later)
    exact = Recurrence(there)
    exact.main_part()
    exact.last_pressure()
    states = exact.states
    first31 = acc.at[pl.ds(0, 31)]
    first32 = acc.at[pl.ds(0, 32)]
    pltpu.make_async_copy(first31, first31, s_recv.at[0]).wait()
    pltpu.make_async_copy(first32, first32, s_recv.at[1]).wait()
    total = jnp.sum(acc[...], axis=0)

    def coefficient(s, r):
        return total[:, s * 4 + r : s * 4 + r + 1]

    chambers = []
    for s in range(4):
        t = coefficient(s, 0)
        for r in range(s):
            t = t + chambers[r] * coefficient(s, r + 1)
        chambers.append(1.5 - 0.5 * (t / NCELLS))
    weights = jnp.where(row2 == 0, 1.0, 0.0)
    for r in range(3):
        weights = jnp.where(row2 == r + 1, chambers[r], weights)

    for layer in range(LAYERS):
        at = pl.ds(layer * PLANE, PLANE)
        for s in range(1, 4):
            walls_ref[s - 1 : s, at] = 0.5 * jnp.sum(weights * states[s][layer], axis=0, keepdims=True)
        pbuf[layer] = jnp.sum(weights * states[4][layer], axis=0, keepdims=True) + 0.2 * chambers[3]
    pout_ref[...] = pbuf[cls]

    each_copy(((0, 3), (1, 2)), lambda copy: copy.wait_send())
    each_rest(lambda copy: copy.wait_send())

    @pl.when(adds)
    def _():
        pltpu.make_async_copy(first31, first31, s_send.at[0]).wait()
        pltpu.make_async_copy(first32, first32, s_send.at[1]).wait()
        pltpu.make_async_copy(first32, first32, s_send.at[2]).wait()
        pltpu.make_async_copy(first31, first31, s_send.at[3]).wait()


def finish_kernel(m_ref, walls_ref, vec_ref, p_ref, out_hbm, pout_hbm, out_v, sem):
    p_out = pltpu.make_async_copy(p_ref, pout_hbm, sem.at[GROUPS])
    p_out.start()
    walls = [
        [jnp.broadcast_to(walls_ref[s : s + 1, i * 128 : (i + 1) * 128], (KC, 128)) for i in range(CHUNKS)]
        for s in range(3)
    ]
    copies = [p_out]
    step = NODES // GROUPS
    for g in range(GROUPS):
        for j in range(g * step, (g + 1) * step):
            at = pl.ds(j * KC, KC)
            v = [vec_ref[s, at, :] for s in range(1, 4)]
            for i in range(CHUNKS):
                y = m_ref[i, at, :]
                for s in range(3):
                    y = y + v[s] * walls[s][i]
                out_v[at, pl.ds(i * 128, 128)] = y
        rows = pl.ds(g * step * KC, step * KC)
        copies.append(pltpu.make_async_copy(out_v.at[rows], out_hbm.at[rows], sem.at[g]))
        copies[-1].start()
    for copy in copies:
        copy.wait()


def shards(melt, counts, pressure, propagator, coupling, flux_weights):
    vmem = pl.BlockSpec(memory_space=pltpu.VMEM)
    hbm = pl.BlockSpec(memory_space=pltpu.HBM)
    dma = pltpu.SemaphoreType.DMA
    m, walls, vec, pout = pl.pallas_call(
        main_kernel,
        name="block_step",
        out_shape=(
            jax.ShapeDtypeStruct((CHUNKS, NODES * KC, 128), F32),
            jax.ShapeDtypeStruct((3, BLOCK), F32),
            jax.ShapeDtypeStruct((4, NODES * KC, 128), F32),
            jax.ShapeDtypeStruct((1, PLANE), F32),
        ),
        in_specs=[hbm] * 6,
        out_specs=(vmem, vmem, vmem, vmem),
        scratch_shapes=[
            pltpu.VMEM((CHUNKS, NODES * KC, 128), F32),
            pltpu.VMEM((KC, BLOCK), jnp.int32),
            pltpu.VMEM((KC * NODES, NODES), F32),
            pltpu.VMEM((KC, NODES), F32),
            pltpu.VMEM((KC, NODES), F32),
            pltpu.VMEM((4, OWN_ROWS, 1, PLANE), F32),
            pltpu.VMEM((3, 4, HALO_ROWS, 1, PLANE), F32),
            pltpu.VMEM((2, HALO_ROWS, 1, PLANE), F32),
            pltpu.VMEM((2, 4, REST_ROWS, 1, PLANE), F32),
            pltpu.VMEM((2, REST_ROWS, 1, PLANE), F32),
            pltpu.VMEM((64, 1, 128), F32),
            pltpu.VMEM((1, 1, 128), F32),
            pltpu.VMEM((LAYERS, 1, PLANE), F32),
            dma((CHUNKS,)), dma((7,)),
            dma((4,)), dma((4,)), dma((2, 4)), dma((2, 4)), dma((2,)), dma((2, 4)),
            dma((4,)), dma((2,)), pltpu.SemaphoreType.REGULAR,
        ],
        compiler_params=pltpu.CompilerParams(collective_id=0, has_side_effects=True, vmem_limit_bytes=32 << 20),
    )(
        *(
            pltpu.with_memory_space_constraint(x, pltpu.HBM)
            for x in (
                melt.reshape(NODES * KC, BLOCK), counts, pressure,
                propagator.reshape(CLASSES * NODES, NODES), coupling, flux_weights,
            )
        )
    )
    shells, pout = pl.pallas_call(
        finish_kernel,
        name="walls_into_shells",
        out_shape=(
            jax.ShapeDtypeStruct((NODES * KC, BLOCK), F32),
            jax.ShapeDtypeStruct((1, PLANE), F32),
        ),
        in_specs=[vmem, vmem, vmem, vmem],
        out_specs=(hbm, hbm),
        scratch_shapes=[pltpu.VMEM((NODES * KC, BLOCK), F32), dma((GROUPS + 1,))],
        compiler_params=pltpu.CompilerParams(vmem_limit_bytes=32 << 20),
    )(m, walls, vec, pout)
    return shells.reshape(NODES, KC, BLOCK), pout


def solution(mesh):
    placed = (P(None, "cls", "cell"), P("cls", "cell"), P(("cell", "cls"), None), P(), P(), P())
    return jax.shard_map(
        shards,
        mesh=mesh,
        in_specs=placed,
        out_specs=(P(None, "cls", "cell"), P(("cell", "cls"), None)),
        check_vma=False,
    )
```

```python
import functools

import jax
import jax.numpy as jnp
from jax import lax
from jax.experimental import pallas as pl
from jax.experimental.pallas import tpu as pltpu
from jax.sharding import PartitionSpec as P

MESH = pl.DeviceIdType.MESH
F32 = jnp.float32
BF16 = jnp.bfloat16
NODES = 64
CLASSES = 32
SIDE = 16
PLANE = 256
LAYERS = 4
BLOCK = LAYERS * PLANE
KC = 8
NCELLS = 65536
COUNT_SCALE = 400.0
CHUNKS = 8
GROUPS = 8
FIRST = 4


HALO = ((0, 1), (1, 1), (2, 1), (3, 1), (5, 1), (0, 2), (1, 2), (3, 2), (1, 3))
REST = ((4, 1), (2, 2), (0, 3))
HALO_ROWS = len(HALO) + 1
REST_ROWS = len(REST)
OWN_ROWS = 8 * LAYERS + 1


def split2(x):
    hi = x.astype(BF16)
    return hi, (x - hi.astype(F32)).astype(BF16)


def dot_nn(a, b):
    return jnp.dot(a, b, preferred_element_type=F32)


def dot3(a, b):
    (ah, al), (bh, bl) = a, b
    return dot_nn(ah, bh) + (dot_nn(al, bh) + dot_nn(ah, bl))


def main_kernel(
    melt_hbm, counts_hbm, pres_ref, prop_hbm, coup_hbm, fw_hbm,
    m_ref, walls_ref, vec_ref, pout_ref,
    melt_v, counts_ref, prop_v, coup_v, fw_v, own, halo, halo_out, rest, rest_out, acc, srow, pbuf,
    load_sem, small_sem, own_send, own_recv, halo_send, halo_recv, rest_send, rest_recv, s_send, s_recv, ready,
):
    cell = lax.axis_index("cell")
    cls = lax.axis_index("cls")
    core = lax.rem(cell, 2)
    yy = lax.rem(lax.div(cell, 2), 4)
    zh = lax.rem(lax.div(cell, 8), 2)
    xx = lax.div(cell, 16)
    has_prev = cell > 0
    has_next = cell < 63

    loads = [
        pltpu.make_async_copy(melt_hbm.at[:, pl.ds(i * 128, 128)], melt_v.at[i], load_sem.at[i])
        for i in range(CHUNKS)
    ]
    smalls = [
        pltpu.make_async_copy(prop_hbm.at[pl.ds(cls * 512, 512)], prop_v, small_sem.at[0]),
        pltpu.make_async_copy(coup_hbm.at[pl.ds(cls * 8, 8)], coup_v, small_sem.at[1]),
        pltpu.make_async_copy(fw_hbm.at[pl.ds(cls * 8, 8)], fw_v, small_sem.at[2]),
        pltpu.make_async_copy(counts_hbm, counts_ref, small_sem.at[3]),
        pltpu.make_async_copy(pres_ref, own.at[cls, OWN_ROWS - 1], small_sem.at[4]),
        pltpu.make_async_copy(pres_ref, halo_out.at[0, HALO_ROWS - 1], small_sem.at[5]),
        pltpu.make_async_copy(pres_ref, halo_out.at[1, HALO_ROWS - 1], small_sem.at[6]),
    ]
    for copy in smalls + loads:
        copy.start()

    barrier = pltpu.get_barrier_semaphore()

    def signal(c, k):
        pl.semaphore_signal(barrier, inc=1, device_id=(c, k), device_id_type=MESH)

    def block_at(x, z, y, c):
        return ((x * 2 + z) * 4 + y) * 2 + c

    adds = jnp.logical_or(cls == 0, cls == 3)
    second = jnp.where(cls == 0, 1, 2)
    near = jnp.where(cls < 2, 3, 0)
    near2 = jnp.where(cls == 3, 1, 2)
    server = jnp.where(cls < 2, 0, 3)
    one = jnp.int32(1)

    @pl.when(has_prev)
    def _():
        for k in range(4):
            signal(cell - 1, k)

    @pl.when(has_next)
    def _():
        for k in range(4):
            signal(cell + 1, k)

    for d in range(4):
        signal(block_at(lax.rem(xx + d, 4), 1 - zh, yy, core), near)
    for d in range(1, 4):
        signal(cell, lax.rem(cls + d, 4))
    for d in range(1, 4):
        signal(block_at(lax.rem(xx + d, 4), zh, yy, core), server)
    for d in range(1, 8):
        signal(lax.div(cell, 8) * 8 + lax.rem(cell + d, 8), cls)

    @pl.when(adds)
    def _():
        for d in range(4):
            signal(block_at(lax.rem(xx + d, 4), 1 - zh, yy, core), near2)
        for d in range(1, 4):
            signal(block_at(lax.rem(xx + d, 4), zh, yy, core), second)

    greeted = 17 + 7 * jnp.where(adds, one, 0) + 4 * jnp.where(has_prev, one, 0) + 4 * jnp.where(has_next, one, 0)

    def own_copy(k):
        return pltpu.make_async_remote_copy(
            src_ref=own.at[cls], dst_ref=own.at[cls], send_sem=own_send.at[k], recv_sem=own_recv.at[cls],
            device_id=(cell, k), device_id_type=MESH)

    def halo_copy(side, k):
        return pltpu.make_async_remote_copy(
            src_ref=halo_out.at[side], dst_ref=halo.at[1 - side, cls], send_sem=halo_send.at[side, k],
            recv_sem=halo_recv.at[1 - side, cls], device_id=(cell + (2 * side - 1), k), device_id_type=MESH)

    def rest_copy(side):
        return pltpu.make_async_remote_copy(
            src_ref=rest_out.at[side], dst_ref=rest.at[1 - side, cls], send_sem=rest_send.at[side],
            recv_sem=rest_recv.at[1 - side, cls], device_id=(cell + (2 * side - 1), 3 - 3 * side), device_id_type=MESH)

    def each_rest(act):
        @pl.when(has_prev)
        def _():
            act(rest_copy(0))

        @pl.when(has_next)
        def _():
            act(rest_copy(1))

    takes_rest = (jnp.logical_and(has_prev, cls == 0), jnp.logical_and(has_next, cls == 3))

    def each_copy(order, act):
        for classes in order:
            @pl.when(has_prev)
            def _(classes=classes):
                for k in classes:
                    act(halo_copy(0, k))

            @pl.when(has_next)
            def _(classes=classes):
                for k in classes:
                    act(halo_copy(1, k))

            for k in classes:
                @pl.when(cls != k)
                def _(k=k):
                    act(own_copy(k))

    for side in range(2):
        @pl.when(jnp.logical_not(takes_rest[side]))
        def _(side=side):
            rest[side] = jnp.zeros((4, REST_ROWS, 1, PLANE), F32)

    halo[2] = jnp.zeros((4, HALO_ROWS, 1, PLANE), F32)
    in_group = lax.rem(cell, 8)
    waits_across = zh == 1
    there = (has_prev, has_next)
    crosses = (jnp.logical_and(has_prev, in_group == 0), jnp.logical_and(has_next, in_group == 7))
    later = tuple(jnp.logical_and(c, waits_across) for c in crosses)
    soon = tuple(jnp.logical_and(t, jnp.logical_not(l)) for t, l in zip(there, later))
    adds_across = jnp.logical_and(jnp.logical_or(crosses[0], crosses[1]), jnp.logical_not(waits_across))
    across_slot = jnp.where(adds_across, jnp.where(crosses[1], 1, 0), 2)

    for copy in smalls:
        copy.wait()
    prop = prop_v[...]
    p_hi, p_lo = split2(prop)
    pp = jnp.concatenate([p_hi, p_lo], axis=1)
    lane = lax.broadcasted_iota(jnp.int32, (KC, 128), 1)
    row = lax.broadcasted_iota(jnp.int32, (KC, 128), 0)
    half = jnp.where(lane >= 64, 1, 0)

    def doubled(x):
        return jnp.concatenate([x, x], axis=1)

    def kron(x):
        return jnp.concatenate([jnp.where(row == 2 * v + half, x, 0.0) for v in range(4)], axis=1)

    def spread(r):
        return jnp.concatenate(split2(kron(r)), axis=0)

    def row_step(wide):
        y = dot_nn(wide, pp)
        y = y[:KC] + y[KC:]
        return y + pltpu.roll(y, 64, 1)

    fw = fw_v[...]
    coup = coup_v[...]
    wide_lane = lax.broadcasted_iota(jnp.int32, (NODES, NODES * KC), 1)
    wide_row = lax.broadcasted_iota(jnp.int32, (NODES, NODES * KC), 0)
    repeat8 = jnp.where(wide_lane // KC == wide_row, 1.0, 0.0).astype(BF16)
    own_class = (wide_lane % KC == wide_row % KC)[: 2 * KC]

    def flux_rows(r):
        both = jnp.concatenate(split2(r[:, :NODES]), axis=0)
        return jnp.where(own_class, dot_nn(both, repeat8), 0.0).astype(BF16)

    rs = [doubled(fw)]
    flux_w = []
    for t in range(4):
        rs.append(row_step(spread(rs[-1])))
        flux_w.append(flux_rows(rs[-1]))
    weights_f = jnp.concatenate(flux_w, axis=0)

    counts_f = counts_ref[...].astype(F32)
    flux = [[] for _ in range(4)]
    for n in range(CHUNKS // 2):
        loads[2 * n].wait()
        loads[2 * n + 1].wait()
        pair = jnp.concatenate([melt_v[2 * n], melt_v[2 * n + 1]], axis=1)
        y = dot_nn(weights_f, pair.astype(BF16))
        for t in range(4):
            flux[t].append(y[16 * t : 16 * t + 8] + y[16 * t + 8 : 16 * t + 16])
    scale = 1.0 / (COUNT_SCALE * CLASSES)

    def put(r, value):
        for l in range(LAYERS):
            tile = value[:, l * PLANE : (l + 1) * PLANE]
            own[cls, r * LAYERS + l] = tile
            if (r, l + 1) in HALO:
                halo_out[0, HALO.index((r, l + 1))] = tile
            if (r, LAYERS - l) in HALO:
                halo_out[1, HALO.index((r, LAYERS - l))] = tile
            if (r, l + 1) in REST:
                rest_out[0, REST.index((r, l + 1))] = tile
            if (r, LAYERS - l) in REST:
                rest_out[1, REST.index((r, LAYERS - l))] = tile

    for t in range(4):
        a_t = jnp.sum(rs[t][:, :NODES] * coup, axis=1, keepdims=True)
        put(2 * t + 1, jnp.sum(counts_f * a_t, axis=0, keepdims=True) * scale)
    for t in range(4):
        put(2 * t, jnp.sum(counts_f * jnp.concatenate(flux[t], axis=1), axis=0, keepdims=True) * scale)

    pl.semaphore_wait(barrier, greeted)
    each_copy(((0, 3),), lambda copy: copy.start())

    def announce(c, k):
        pl.semaphore_signal(ready, inc=1, device_id=(c, k), device_id_type=MESH)

    for d in range(1, 4):
        announce(block_at(lax.rem(xx + d, 4), zh, yy, core), server)
    for d in range(4):
        announce(block_at(lax.rem(xx + d, 4), 1 - zh, yy, core), near)

    @pl.when(jnp.logical_not(adds))
    def _():
        announce(cell, server)

    def col_step(v):
        hi, lo = split2(v[:, :NODES])
        lhs = jnp.concatenate([hi, lo], axis=0)
        nt = (((1,), (1,)), ((), ()))
        y = lax.dot_general(lhs, p_hi, nt, preferred_element_type=F32)
        y = y[:KC] + y[KC:] + lax.dot_general(hi, p_lo, nt, preferred_element_type=F32)
        z = jnp.zeros((KC, 128), F32)
        for q in range(4):
            z = z + jnp.where(row == 2 * q + half, y[:, 128 * q : 128 * (q + 1)], 0.0)
        return z + pltpu.roll(z, 64, 1)

    vs = [doubled(coup)]
    for s in range(3):
        vs.append(col_step(vs[-1]))
    for s in range(4):
        for j in range(NODES):
            vec_ref[s, pl.ds(j * KC, KC), :] = jnp.broadcast_to(vs[3 - s][:, j : j + 1], (KC, 128))

    def powers_into_melt(classes):
        for k in classes:
            base = split2(prop_v[pl.ds(k * NODES, NODES), :])
            two = split2(dot3(base, base))
            four_hi, four_lo = split2(dot3(two, two))
            lhs = jnp.concatenate([four_hi, four_hi, four_lo], axis=1)
            at = pl.ds(k, NODES, stride=KC)
            for n in range(CHUNKS // 2):
                x = jnp.concatenate([melt_v[2 * n, at, :], melt_v[2 * n + 1, at, :]], axis=1)
                x_hi, x_lo = split2(x)
                y = dot_nn(lhs, jnp.concatenate([x_hi, x_lo, x_hi], axis=0))
                m_ref[2 * n, at, :] = y[:, :128]
                m_ref[2 * n + 1, at, :] = y[:, 128:]

    powers_into_melt(range(0, 3))
    each_copy(((1, 2),), lambda copy: copy.start())
    each_rest(lambda copy: copy.start())
    powers_into_melt(range(3, FIRST))

    for d in range(1, 4):
        k = lax.rem(cls + d, 4)
        pltpu.make_async_copy(own.at[k], own.at[k], own_recv.at[k]).wait()
    def wait_halo(sides):
        for side in range(2):
            @pl.when(sides[side])
            def _(side=side):
                for k in range(4):
                    pltpu.make_async_copy(halo.at[side, k], halo.at[side, k], halo_recv.at[side, k]).wait()

    wait_halo(soon)

    lane2 = lax.broadcasted_iota(jnp.int32, (KC, PLANE), 1)
    row2 = lax.broadcasted_iota(jnp.int32, (KC, PLANE), 0)

    def plane_neighbours(x):
        west = jnp.where(lane2 % SIDE == 0, 0.0, pltpu.roll(x, 1, 1))
        east = jnp.where(lane2 % SIDE == SIDE - 1, 0.0, pltpu.roll(x, PLANE - 1, 1))
        north = jnp.where(lane2 < SIDE, 0.0, pltpu.roll(x, SIDE, 1))
        south = jnp.where(lane2 >= PLANE - SIDE, 0.0, pltpu.roll(x, PLANE - SIDE, 1))
        return west + east + (north + south)

    def halo_field(slot, r, d):
        rows = [halo[slot, k, HALO.index((r, d))] for k in range(4)]
        return jnp.broadcast_to(rows[0] + rows[1] + (rows[2] + rows[3]), (KC, PLANE))

    class Recurrence:
        def __init__(self, sides):
            self.slots = [jnp.where(sides[side], side, 2) for side in range(2)]
            self.inside = [jnp.where(sides[side], 1.0, 0.0).astype(F32) for side in range(2)]
            self.fields = {}
            self.gases = [{} for _ in range(4)]
            self.states = [{} for _ in range(5)]
            for layer in range(-4, 8):
                p = jnp.broadcast_to(self.start_pressure(layer), (KC, PLANE))
                self.states[0][layer] = jnp.where(row2 == 0, p, 0.0)

        def start_pressure(self, layer):
            if 0 <= layer < LAYERS:
                return own[layer, OWN_ROWS - 1]
            side, k = (0, layer + 4) if layer < 0 else (1, layer - LAYERS)
            return halo[self.slots[side], k, HALO_ROWS - 1]

        def field(self, layer, r):
            if (layer, r) not in self.fields:
                if 0 <= layer < LAYERS:
                    rows = [own[k, r * LAYERS + layer] for k in range(4)]
                    value = jnp.broadcast_to(rows[0] + rows[1] + (rows[2] + rows[3]), (KC, PLANE))
                else:
                    side, d = (0, -layer) if layer < 0 else (1, layer - LAYERS + 1)
                    if (r, d) in HALO:
                        value = halo_field(self.slots[side], r, d)
                    else:
                        rows = [rest[side, k, REST.index((r, d))] for k in range(4)]
                        value = jnp.broadcast_to(rows[0] + rows[1] + (rows[2] + rows[3]), (KC, PLANE))
                self.fields[layer, r] = value
            return self.fields[layer, r]

        def add_gas(self, s, layers):
            for layer in layers:
                g = jnp.where(row2 == 0, self.field(layer, 2 * s), 0.0)
                for m in range(s + 1):
                    g = g + self.field(layer, 2 * m + 1) * (0.5 * self.states[s - m][layer])
                self.gases[s][layer] = g

        def advance(self, s, layers):
            now = self.states[s]
            for layer in layers:
                x = now[layer]
                around = plane_neighbours(x) + (now[layer - 1] + now[layer + 1])
                x = x + 0.15 * (around - 6.0 * x) + 0.1 * self.gases[s][layer] - 0.2 * x
                x = x + jnp.where(row2 == s + 1, 0.2, 0.0)
                if layer < 0:
                    x = x * self.inside[0]
                if layer >= LAYERS:
                    x = x * self.inside[1]
                self.states[s + 1][layer] = x

        def main_part(self):
            for s in range(3):
                reach = range(s - 2, LAYERS + 2 - s)
                self.add_gas(s, reach)
                self.advance(s, reach)
            self.add_gas(3, range(LAYERS))

        def last_pressure(self):
            for s in range(3):
                ends = (s - 3, LAYERS + 2 - s)
                self.add_gas(s, ends)
                self.advance(s, ends)
            self.advance(3, range(LAYERS))

    quick = Recurrence(soon)
    quick.main_part()
    gases = quick.gases

    extra = [{} for _ in range(4)]
    shift = [{} for _ in range(4)]
    for s in range(1, 4):
        for d in range(1, s + 1):
            if d == 1:
                inner = jnp.where(crosses[1], quick.states[s - 1][LAYERS - 1], quick.states[s - 1][0])
            else:
                inner = shift[s - 1][d - 1]
            y = 0.15 * inner
            if d in shift[s - 1]:
                x = shift[s - 1][d]
                around = plane_neighbours(x)
                if d + 1 in shift[s - 1]:
                    around = around + shift[s - 1][d + 1]
                y = y + (x + 0.15 * (around - 6.0 * x) + 0.1 * extra[s - 1][d] - 0.2 * x)
            shift[s][d] = y
            g = jnp.zeros((KC, PLANE), F32)
            for m in range(s):
                if d in shift[s - m]:
                    g = g + halo_field(across_slot, 2 * m + 1, d) * (0.5 * shift[s - m][d])
            extra[s][d] = g

    packed = jnp.zeros((KC, 128), F32)
    for s in range(4):
        t = gases[s][0] + gases[s][1] + (gases[s][2] + gases[s][3])
        for d in extra[s]:
            t = t + extra[s][d]
        t = jnp.sum(t[:, :128] + t[:, 128:], axis=1, keepdims=True)
        packed = packed + jnp.where(jnp.logical_and(lane == s * 4 + row, row < 4), t, 0.0)
    packed = jnp.sum(packed, axis=0, keepdims=True)
    slot = (xx * 4 + yy) * 2 + core
    srow[0] = packed
    acc[zh * 32 + slot] = packed

    hops = [0, 1, 2, 1]
    offsets = sorted(
        ((dx, dy, dc) for dx in range(4) for dy in range(4) for dc in range(2)),
        key=lambda o: -(hops[o[0]] + hops[o[1]] + 0.3 * o[2]),
    )

    def block_of(o, z):
        return block_at(lax.rem(xx + o[0], 4), z, lax.rem(yy + o[1], 4), lax.rem(core + o[2], 2))

    def sum_copy(c, k, sem, arrived):
        return pltpu.make_async_remote_copy(
            src_ref=srow.at[0], dst_ref=acc.at[zh * 32 + slot], send_sem=sem, recv_sem=arrived,
            device_id=(c, k), device_id_type=MESH)

    @pl.when(adds)
    def _():
        pl.semaphore_wait(ready, 15)
        for o in offsets:
            sum_copy(block_of(o, 1 - zh), near2, s_send.at[2], s_recv.at[1]).start()
            sum_copy(block_of(o, 1 - zh), near, s_send.at[1], s_recv.at[1]).start()
            if o != (0, 0, 0):
                sum_copy(block_of(o, zh), second, s_send.at[3], s_recv.at[0]).start()
                sum_copy(block_of(o, zh), cls, s_send.at[0], s_recv.at[0]).start()

    powers_into_melt(range(FIRST, KC))
    for side in range(2):
        @pl.when(takes_rest[side])
        def _(side=side):
            for k in range(4):
                pltpu.make_async_copy(rest.at[side, k], rest.at[side, k], rest_recv.at[side, k]).wait()

    for i in range(CHUNKS):
        l, part_of = divmod(i * 128, PLANE)
        wall = jnp.broadcast_to(0.5 * own[l, OWN_ROWS - 1][:, part_of : part_of + 128], (KC, 128))

        def first_wall(j, carry, i=i, wall=wall):
            at = pl.ds(pl.multiple_of(j * KC, KC), KC)
            m_ref[i, at, :] = m_ref[i, at, :] + vec_ref[0, at, :] * wall
            return carry

        lax.fori_loop(0, NODES, first_wall, 0, unroll=16)

    wait_halo(later)
    exact = Recurrence(there)
    exact.main_part()
    exact.last_pressure()
    states = exact.states
    first31 = acc.at[pl.ds(0, 31)]
    first32 = acc.at[pl.ds(0, 32)]
    each_copy(((0, 3), (1, 2)), lambda copy: copy.wait_send())
    each_rest(lambda copy: copy.wait_send())

    @pl.when(adds)
    def _():
        pltpu.make_async_copy(first31, first31, s_send.at[0]).wait()
        pltpu.make_async_copy(first32, first32, s_send.at[1]).wait()
        pltpu.make_async_copy(first32, first32, s_send.at[2]).wait()
        pltpu.make_async_copy(first31, first31, s_send.at[3]).wait()

    pltpu.make_async_copy(first31, first31, s_recv.at[0]).wait()
    pltpu.make_async_copy(first32, first32, s_recv.at[1]).wait()
    total = jnp.sum(acc[...], axis=0)

    def coefficient(s, r):
        return total[:, s * 4 + r : s * 4 + r + 1]

    chambers = []
    for s in range(4):
        t = coefficient(s, 0)
        for r in range(s):
            t = t + chambers[r] * coefficient(s, r + 1)
        chambers.append(1.5 - 0.5 * (t / NCELLS))
    weights = jnp.where(row2 == 0, 1.0, 0.0)
    for r in range(3):
        weights = jnp.where(row2 == r + 1, chambers[r], weights)

    for layer in range(LAYERS):
        at = pl.ds(layer * PLANE, PLANE)
        for s in range(1, 4):
            walls_ref[s - 1 : s, at] = 0.5 * jnp.sum(weights * states[s][layer], axis=0, keepdims=True)
        pbuf[layer] = jnp.sum(weights * states[4][layer], axis=0, keepdims=True) + 0.2 * chambers[3]
    pout_ref[...] = pbuf[cls]


def finish_kernel(m_ref, walls_ref, vec_ref, p_ref, out_hbm, pout_hbm, out_v, sem):
    p_out = pltpu.make_async_copy(p_ref, pout_hbm, sem.at[GROUPS])
    p_out.start()
    walls = [
        [jnp.broadcast_to(walls_ref[s : s + 1, i * 128 : (i + 1) * 128], (KC, 128)) for i in range(CHUNKS)]
        for s in range(3)
    ]
    copies = [p_out]
    step = NODES // GROUPS
    for g in range(GROUPS):
        for j in range(g * step, (g + 1) * step):
            at = pl.ds(j * KC, KC)
            v = [vec_ref[s, at, :] for s in range(1, 4)]
            for i in range(CHUNKS):
                y = m_ref[i, at, :]
                for s in range(3):
                    y = y + v[s] * walls[s][i]
                out_v[at, pl.ds(i * 128, 128)] = y
        rows = pl.ds(g * step * KC, step * KC)
        copies.append(pltpu.make_async_copy(out_v.at[rows], out_hbm.at[rows], sem.at[g]))
        copies[-1].start()
    for copy in copies:
        copy.wait()


def shards(melt, counts, pressure, propagator, coupling, flux_weights):
    vmem = pl.BlockSpec(memory_space=pltpu.VMEM)
    hbm = pl.BlockSpec(memory_space=pltpu.HBM)
    dma = pltpu.SemaphoreType.DMA
    m, walls, vec, pout = pl.pallas_call(
        main_kernel,
        name="block_step",
        out_shape=(
            jax.ShapeDtypeStruct((CHUNKS, NODES * KC, 128), F32),
            jax.ShapeDtypeStruct((3, BLOCK), F32),
            jax.ShapeDtypeStruct((4, NODES * KC, 128), F32),
            jax.ShapeDtypeStruct((1, PLANE), F32),
        ),
        in_specs=[hbm] * 6,
        out_specs=(vmem, vmem, vmem, vmem),
        scratch_shapes=[
            pltpu.VMEM((CHUNKS, NODES * KC, 128), F32),
            pltpu.VMEM((KC, BLOCK), jnp.int32),
            pltpu.VMEM((KC * NODES, NODES), F32),
            pltpu.VMEM((KC, NODES), F32),
            pltpu.VMEM((KC, NODES), F32),
            pltpu.VMEM((4, OWN_ROWS, 1, PLANE), F32),
            pltpu.VMEM((3, 4, HALO_ROWS, 1, PLANE), F32),
            pltpu.VMEM((2, HALO_ROWS, 1, PLANE), F32),
            pltpu.VMEM((2, 4, REST_ROWS, 1, PLANE), F32),
            pltpu.VMEM((2, REST_ROWS, 1, PLANE), F32),
            pltpu.VMEM((64, 1, 128), F32),
            pltpu.VMEM((1, 1, 128), F32),
            pltpu.VMEM((LAYERS, 1, PLANE), F32),
            dma((CHUNKS,)), dma((7,)),
            dma((4,)), dma((4,)), dma((2, 4)), dma((2, 4)), dma((2,)), dma((2, 4)),
            dma((4,)), dma((2,)), pltpu.SemaphoreType.REGULAR,
        ],
        compiler_params=pltpu.CompilerParams(collective_id=0, has_side_effects=True, vmem_limit_bytes=32 << 20),
    )(
        *(
            pltpu.with_memory_space_constraint(x, pltpu.HBM)
            for x in (
                melt.reshape(NODES * KC, BLOCK), counts, pressure,
                propagator.reshape(CLASSES * NODES, NODES), coupling, flux_weights,
            )
        )
    )
    shells, pout = pl.pallas_call(
        finish_kernel,
        name="walls_into_shells",
        out_shape=(
            jax.ShapeDtypeStruct((NODES * KC, BLOCK), F32),
            jax.ShapeDtypeStruct((1, PLANE), F32),
        ),
        in_specs=[vmem, vmem, vmem, vmem],
        out_specs=(hbm, hbm),
        scratch_shapes=[pltpu.VMEM((NODES * KC, BLOCK), F32), dma((GROUPS + 1,))],
        compiler_params=pltpu.CompilerParams(vmem_limit_bytes=32 << 20),
    )(m, walls, vec, pout)
    return shells.reshape(NODES, KC, BLOCK), pout


def solution(mesh):
    placed = (P(None, "cls", "cell"), P("cls", "cell"), P(("cell", "cls"), None), P(), P(), P())
    return jax.shard_map(
        shards,
        mesh=mesh,
        in_specs=placed,
        out_specs=(P(None, "cls", "cell"), P(("cell", "cls"), None)),
        check_vma=False,
    )
```
